32 devices in a mesh: groups: 2 (over y), chol: 4 (over z), walk: 4 (over x, core).
Axes of the slice: x: 2, y: 2, z: 4, core: 2. Of those that a mesh axis runs over, the one named last changes fastest.
Arguments:
- green: bfloat16 [8, 200, 1600], P(('groups', 'walk')), parts along dimension 0, may hold values from -2 to 2
- chol: bfloat16 [16, 200, 1600], P(('groups', 'chol')), parts along dimension 0, may hold values from -0.19921875 to 0.19921875
- trial: bfloat16 [3200, 200], P(('groups', 'chol')), parts along dimension 0, may hold values from -1.1953125 to 1.1953125
- hamil: bfloat16 [1600, 1600], P('chol'), may hold values from -0.21875 to 0.21875
- energy_cot: float32 [8], P('groups'), parts along dimension 0, may hold values from -4 to 4
Outputs:
- d_green: float32 [8, 200, 1600], P(('groups', 'walk'), None, 'chol'), parts along dimension 0
- d_chol: float32 [16, 200, 1600], P(('groups', 'chol'), None, 'walk'), parts along dimension 0
- d_trial: float32 [3200, 200], P(('groups', 'chol')), parts along dimension 0
The draws below stay inside these ranges and needn't reach their ends.
There are 2 independent parts, one for each index of `groups`. The reference program is written for one: setup_inputs(seed, part) draws one part's arguments, and reference() takes and returns one part's arrays. A program takes and returns all parts, laid end to end along the dimension named above; an argument that names none is the same for every part. Nothing has to cross between parts.
All inputs are finite; a program needn't handle non-finite values.
Results may differ from the reference program's by a relative error of at most 0.0029.
Values may be sent and summed in bfloat16 or wider, within the bound.
A program may use at most 64 MiB of HBM per device.

```python
import jax
import jax.numpy as jnp
from jax import lax

NOCC = 200
NORB = 1600
NCHOL = 8
NWALK = 4


def raised(result, own_key, source, target, blocks, factor):
    owner, partner = [(jnp.arange(result.shape[position]) // (result.shape[position] // blocks)).reshape([-1 if axis == position else 1 for axis in range(result.ndim)]) for position in (source, target)]
    chosen = jax.random.permutation(own_key, blocks)[partner]
    strong = (owner == chosen) | (owner == (partner + blocks // 2) % blocks)
    return jnp.where(strong, factor * result, result)


def block_scale(rng, dims, pieces, low, largest):
    def one(position, shards_of):
        heights = jax.random.uniform(jax.random.fold_in(jax.random.fold_in(rng, 6), position), (shards_of,), jnp.float32, low / len(pieces), largest / len(pieces))
        return jnp.repeat(jnp.exp(heights), dims[position] // shards_of).reshape((-1,) + (1,) * (len(dims) - position - 1))

    level = one(*pieces[0])
    for cut in pieces[1:]:
        level = level * one(*cut)
    return level


def centred(rng, extent, deviation, limit, cuts=(), kind=jnp.bfloat16):
    array = jax.random.normal(rng, extent, jnp.float32) * deviation
    if len(cuts) > 0:
        array = block_scale(rng, extent, cuts, -0.22, 0.18) * array
    return jnp.clip(array, min=-limit, max=limit).astype(kind)


def bell_draw_with(key, shape, width, most, cuts, heavy, kind=jnp.bfloat16):
    array = width * jax.random.normal(key, shape, jnp.float32)
    if cuts:
        array = array * block_scale(key, shape, cuts, -0.22, 0.18)
    return jnp.clip(raised(array, jax.random.fold_in(key, 3), *heavy), -most, most).astype(kind)


def setup_inputs(seed: int = 0, part: int = 0) -> dict:
    key_of = jax.random.split(jax.random.key(seed), 6)
    part_splits = jax.random.split(jax.random.fold_in(key_of[5], part), 6)
    green = centred(part_splits[0], (NWALK, NOCC, NORB), 0.3, 2.0, ((0, 4),))
    chol = bell_draw_with(part_splits[1], (NCHOL, NOCC, NORB), 0.02, 0.19921875, ((0, 4),), (0, 2, 4, 2.0))
    trial = centred(part_splits[2], (NORB, NOCC), 0.2, 1.1953125, ((0, 4),))
    hamil = bell_draw_with(key_of[3], (NORB, NORB), NORB ** -0.5, 0.21875, ((0, 4),), (0, 1, 4, 2.0))
    energy_cot = centred(part_splits[4], (NWALK,), 1.0, 4.0, (), jnp.float32)
    return dict(green=green, chol=chol, trial=trial, hamil=hamil, energy_cot=energy_cot)


def reference(green, chol, trial, hamil, energy_cot):
    green_f32 = green.astype(jnp.float32)
    hrot = jnp.dot(trial.T, hamil, preferred_element_type=jnp.float32)
    identity = jnp.eye(NOCC, dtype=jnp.float32)

    def accumulate(total, slab_vec):
        slab_f32 = slab_vec.astype(jnp.float32)
        coulomb = jnp.einsum("wip,ip->w", green_f32, slab_f32)
        exchange_mat = jnp.einsum("ip,wjp->wij", slab_f32, green_f32)
        kernel_mat = (energy_cot[:, None, None] * (coulomb[:, None, None] * identity - exchange_mat)).astype(jnp.bfloat16)
        kernel_f32 = lax.optimization_barrier(kernel_mat).astype(jnp.float32)
        slab_grad = jnp.einsum("wji,wjp->ip", kernel_f32, green_f32)
        total = total + jnp.einsum("wij,jp->wip", kernel_f32, slab_f32)
        return total, slab_grad

    start_total = energy_cot[:, None, None] * hrot[None]
    d_green, d_chol = lax.scan(accumulate, start_total, chol)
    gbar = jnp.einsum("w,wip->ip", energy_cot, green_f32, precision=lax.Precision.HIGHEST).astype(jnp.bfloat16)
    d_trial = jnp.dot(hamil, gbar.T, preferred_element_type=jnp.float32)
    return d_green, d_chol, d_trial
```

```python
import functools

import jax
import jax.numpy as jnp
from jax import lax
from jax.experimental import pallas as pl
from jax.experimental.pallas import tpu as pltpu
from jax.sharding import PartitionSpec as P

MESH = pl.DeviceIdType.MESH
F32 = jnp.float32
BF16 = jnp.bfloat16


def nt(a, b):
    return lax.dot_general(a, b, (((1,), (1,)), ((), ())), preferred_element_type=F32)


def nn(a, b):
    return lax.dot_general(a, b, (((1,), (0,)), ((), ())), preferred_element_type=F32)


def tn(a, b):
    return lax.dot_general(a, b, (((0,), (0,)), ((), ())), preferred_element_type=F32)


def kernel_of(exchange, cot):
    rows = lax.broadcasted_iota(jnp.int32, exchange.shape, 0)
    cols = lax.broadcasted_iota(jnp.int32, exchange.shape, 1)
    diagonal = rows == cols
    coulomb = jnp.sum(jnp.where(diagonal, exchange, 0.0))
    return (cot * (jnp.where(diagonal, coulomb, 0.0) - exchange)).astype(BF16)


def row_chunks(rows, count):
    step = rows // count // 16 * 16
    starts = [k * step for k in range(count)]
    return [(s, e - s) for s, e in zip(starts, starts[1:] + [rows])]


def body(
    chunks, cot_ref, green_hbm, chol_hbm, trial_hbm, hamil_hbm,
    dgreen_ref, dchol_ref, dtrial_ref,
    green_ref, chol_ref, trial_ref, hamil_ref,
    quarters, peer_quarters, kernels, peer_kernels,
    held, outbox, inbox, foldbox, chol_out, chol_in,
    part, part_in, trial_out, trial_in,
    load_sem, quarter_send, quarter_recv, kernel_send, kernel_recv,
    chol_send, chol_recv, part_send, part_recv, trial_send, trial_recv, done_send, done_recv,
    z_send, z_recv, fold_send, fold_recv, forward_send, forward_recv,
):
    n_walk, n_chol = 4, 4
    walk = lax.axis_index("walk")
    rank = lax.axis_index("chol")
    n_vec, occ, orb = chol_ref.shape
    core = walk % 2
    mate = walk + 1 - 2 * core
    across = (walk + 2) % n_walk
    quarter = orb // n_walk
    third = orb // n_chol
    half = hamil_ref.shape[0] // 2
    folds = {(0, 3): 1, (3, 0): 2}

    loads = [
        pltpu.make_async_copy(source, target, load_sem.at[k])
        for k, (source, target) in enumerate((
            (green_hbm.at[0], green_ref), (chol_hbm, chol_ref),
            (trial_hbm, trial_ref), (hamil_hbm, hamil_ref),
        ))
    ]
    for load in loads:
        load.start()
    barrier = pltpu.get_barrier_semaphore()
    for device in (mate, across):
        pl.semaphore_signal(barrier, inc=1, device_id={"walk": device}, device_id_type=MESH)

    def remote(source, target, send, recv, axis, device):
        return pltpu.make_async_remote_copy(
            source, target, send, recv, device_id={axis: device}, device_id_type=MESH
        )

    def to_mate_quarter(k):
        index = mate if k == 0 else (mate + 2) % n_walk
        return remote(
            quarters.at[index], peer_quarters.at[k], quarter_send.at[k], quarter_recv.at[k],
            "walk", mate,
        )

    def to_mate_kernel(g):
        return remote(
            kernels.at[g], peer_kernels.at[g], kernel_send.at[g], kernel_recv.at[g], "walk", mate
        )

    def to_across_chol(g):
        return remote(
            chol_out.at[g], chol_in.at[g], chol_send.at[g], chol_recv.at[g], "walk", across
        )

    def rows_of(side):
        return pl.ds(pl.multiple_of(side * half, 8), half)

    def to_mate_part():
        return remote(part.at[rows_of(1 - core)], part_in, part_send, part_recv, "walk", mate)

    def to_across_trial():
        return remote(trial_out, trial_in, trial_send, trial_recv, "walk", across)

    def to_mate_done(side):
        span = rows_of(side)
        return remote(
            dtrial_ref.at[span], dtrial_ref.at[span], done_send, done_recv, "walk", mate
        )

    def to_z(r, c):
        return remote(outbox.at[c], inbox.at[r], z_send.at[c], z_recv.at[r], "chol", c)

    def to_fold(c, k, middle):
        span = pl.ds(*chunks[k])
        return remote(
            outbox.at[c, span], foldbox.at[span], fold_send.at[k], fold_recv.at[k],
            "chol", middle,
        )

    def forward(r, c, k):
        span = pl.ds(*chunks[k])
        return remote(
            outbox.at[c, span], inbox.at[r, span], forward_send.at[k], forward_recv.at[k],
            "chol", c,
        )

    def window(c):
        low = c * third // 128 * 128
        high = min(orb, -(-(c + 1) * third // 128) * 128)
        total = cot * tn(trial_ref[...], hamil_ref[:, low:high])
        for g in range(n_vec):
            total = total + nn(kernels[g], chol_ref[g, :, low:high])
        return total[:, c * third - low:(c + 1) * third - low]

    def send_piece(r, c):
        piece = window(c)
        if (r, c) in folds:
            outbox[c] = piece.astype(BF16)
            for k in range(len(chunks)):
                to_fold(c, k, folds[r, c]).start()
        elif r in [middle for (_, end), middle in folds.items() if end == c]:
            held[...] = piece
        else:
            outbox[c] = piece.astype(BF16)
            to_z(r, c).start()

    loads[0].wait()
    for q in range(n_walk):
        quarters[q] = green_ref[:, q * quarter:(q + 1) * quarter]
    cot = cot_ref[walk]
    loads[1].wait()
    kernels[0] = kernel_of(nt(chol_ref[0], green_ref[...]), cot)

    for r in range(n_chol):

        @pl.when(rank == r)
        def _():
            pl.semaphore_wait(barrier, 2 + (r > 0))
            for c in (r + 1, r - 1, r - 2):
                if 0 <= c < n_chol:
                    pl.semaphore_signal(
                        barrier, inc=1, device_id={"chol": c}, device_id_type=MESH
                    )

    to_mate_quarter(1).start()
    to_mate_kernel(0).start()
    for g in range(1, n_vec):
        kernels[g] = kernel_of(nt(chol_ref[g], green_ref[...]), cot)
        to_mate_kernel(g).start()
    to_mate_quarter(0).start()
    loads[2].wait()
    loads[3].wait()

    for r, order in ((1, (0,)), (2, (1, 0)), (3, (0, 1, 2))):

        @pl.when(rank == r)
        def _():
            for c in order:
                send_piece(r, c)

    part[...] = cot * nt(hamil_ref[...], green_ref[...])
    to_mate_part().start()
    to_mate_quarter(1).wait_recv()
    for g in range(n_vec):
        to_mate_kernel(g).wait_recv()
        if g == n_vec - 1:
            to_mate_part().wait_recv()
            part_in[...] += part[rows_of(core), :]
            trial_out[...] = part_in[...].astype(BF16)
            to_across_trial().start()
        chol_out[g] = (
            tn(kernels[g], quarters[across]) + tn(peer_kernels[g], peer_quarters[1])
        ).astype(BF16)
        to_across_chol(g).start()

    for r, order in ((0, (3, 2, 1)), (1, (2, 3)), (2, (3,))):

        @pl.when(rank == r)
        def _():
            pl.semaphore_wait(barrier, min(2, n_chol - 1 - r))
            for c in order:
                send_piece(r, c)

    for r in range(n_chol):

        @pl.when(rank == r)
        def _():
            dgreen_ref[0] = window(r)

    to_mate_quarter(0).wait_recv()
    for g in range(n_vec):
        dchol_ref[g] = tn(kernels[g], quarters[walk]) + tn(peer_kernels[g], peer_quarters[0])

    for (start, end), middle in folds.items():

        @pl.when(rank == middle)
        def _():
            for k, (first, count) in enumerate(chunks):
                span = pl.ds(first, count)
                to_fold(end, k, middle).wait_recv()
                outbox[end, span, :] = (
                    held[span, :] + foldbox[span, :].astype(F32)
                ).astype(BF16)
                forward(middle, end, k).start()

    for g in range(n_vec):
        if g == n_vec - 1:
            to_across_trial().wait_recv()
            dtrial_ref[rows_of(core), :] = part_in[...] + trial_in[...].astype(F32)
            to_mate_done(core).start()
        to_across_chol(g).wait_recv()
        dchol_ref[g] += chol_in[g].astype(F32)

    for r, order in ((0, (1, 2)), (1, (2, 0, 3)), (2, (1, 0, 3)), (3, (2, 1))):

        @pl.when(rank == r)
        def _():
            for c in order:
                if c in [middle for (_, end), middle in folds.items() if end == r]:
                    for k, (first, count) in enumerate(chunks):
                        span = pl.ds(first, count)
                        forward(c, r, k).wait_recv()
                        dgreen_ref[0, span, :] += inbox[c, span, :].astype(F32)
                else:
                    to_z(c, r).wait_recv()
                    dgreen_ref[0] += inbox[c].astype(F32)

    to_mate_done(1 - core).wait_recv()

    for k in range(2):
        to_mate_quarter(k).wait_send()
    for g in range(n_vec):
        to_mate_kernel(g).wait_send()
        to_across_chol(g).wait_send()
    to_mate_part().wait_send()
    to_across_trial().wait_send()
    to_mate_done(core).wait_send()
    for r in range(n_chol):

        @pl.when(rank == r)
        def _():
            for c in range(n_chol):
                if c == r:
                    continue
                for k in range(len(chunks)):
                    if (r, c) in folds:
                        to_fold(c, k, folds[r, c]).wait_send()
                    elif r in [middle for (_, end), middle in folds.items() if end == c]:
                        forward(r, c, k).wait_send()
                    elif k == 0:
                        to_z(r, c).wait_send()


def write_out(*refs):
    sources, targets, sem = refs[:3], refs[3:6], refs[6]
    copies = [pltpu.make_async_copy(s, t, sem.at[k]) for k, (s, t) in enumerate(zip(sources, targets))]
    for copy in copies:
        copy.start()
    for copy in copies:
        copy.wait()


def fused(green, chol, trial, hamil, energy_cot):
    n_chol = lax.axis_size("chol")
    n_walk = lax.axis_size("walk")
    _, occ, orb = green.shape
    n_vec = chol.shape[0]
    rows = hamil.shape[0]
    chunks = row_chunks(occ, 2)
    vmem = pl.BlockSpec(memory_space=pltpu.VMEM)
    anywhere = pl.BlockSpec(memory_space=pl.ANY)
    dma = pltpu.SemaphoreType.DMA
    shapes = [
        (1, occ, orb // n_chol),
        (n_vec, occ, orb // n_walk),
        (rows, occ),
    ]
    results = pl.pallas_call(
        functools.partial(body, chunks),
        out_shape=tuple(pltpu.VMEM(shape, F32) for shape in shapes),
        in_specs=[pl.BlockSpec(memory_space=pltpu.SMEM)] + [anywhere] * 4,
        out_specs=(vmem,) * 3,
        scratch_shapes=[
            pltpu.VMEM((occ, orb), BF16),
            pltpu.VMEM(chol.shape, BF16),
            pltpu.VMEM(trial.shape, BF16),
            pltpu.VMEM(hamil.shape, BF16),
            pltpu.VMEM((n_walk, occ, orb // n_walk), BF16),
            pltpu.VMEM((2, occ, orb // n_walk), BF16),
            pltpu.VMEM((n_vec, occ, occ), BF16),
            pltpu.VMEM((n_vec, occ, occ), BF16),
            pltpu.VMEM((occ, orb // n_chol), F32),
            pltpu.VMEM((n_chol, occ, orb // n_chol), BF16),
            pltpu.VMEM((n_chol, occ, orb // n_chol), BF16),
            pltpu.VMEM((occ, orb // n_chol), BF16),
            pltpu.VMEM((n_vec, occ, orb // n_walk), BF16),
            pltpu.VMEM((n_vec, occ, orb // n_walk), BF16),
            pltpu.VMEM((rows, occ), F32),
            pltpu.VMEM((rows // 2, occ), F32),
            pltpu.VMEM((rows // 2, occ), BF16),
            pltpu.VMEM((rows // 2, occ), BF16),
            dma((4,)), dma((2,)), dma((2,)), dma((n_vec,)), dma((n_vec,)),
            dma((n_vec,)), dma((n_vec,)), dma, dma, dma, dma, dma, dma,
            dma((n_chol,)), dma((n_chol,)),
            dma((len(chunks),)), dma((len(chunks),)), dma((len(chunks),)), dma((len(chunks),)),
        ],
        compiler_params=pltpu.CompilerParams(
            collective_id=0, has_side_effects=True, vmem_limit_bytes=60 * 1024 * 1024
        ),
    )(energy_cot, green, chol, trial, hamil)
    return pl.pallas_call(
        write_out,
        out_shape=tuple(jax.ShapeDtypeStruct(shape, F32) for shape in shapes),
        in_specs=[anywhere] * 3,
        out_specs=(anywhere,) * 3,
        scratch_shapes=[dma((3,))],
        compiler_params=pltpu.CompilerParams(vmem_limit_bytes=1024 * 1024),
    )(*results)


def shards(green, chol, trial, hamil, energy_cot):
    walk_rank = lax.axis_index("walk")
    walk_rows = green.shape[0]
    cot_own = lax.dynamic_slice_in_dim(energy_cot, walk_rank * walk_rows, walk_rows, 0)
    hrot_part = lax.dot_general(
        trial, hamil, (((0,), (0,)), ((), ())), preferred_element_type=jnp.float32
    )
    identity = jnp.eye(trial.shape[1], dtype=jnp.float32)
    quarter = green.shape[2] // lax.axis_size("walk")
    greens = lax.all_gather(green, "walk", axis=0, tiled=True)
    coulomb = jnp.einsum("cip,wip->cw", chol, greens, preferred_element_type=jnp.float32)
    exchange_mat = jnp.einsum("cip,wjp->cwij", chol, greens, preferred_element_type=jnp.float32)
    kernel_mat = (
        energy_cot[None, :, None, None] * (coulomb[:, :, None, None] * identity - exchange_mat)
    ).astype(jnp.bfloat16)
    kernel_own = lax.dynamic_slice_in_dim(kernel_mat, walk_rank * walk_rows, walk_rows, 1)
    green_part = jnp.einsum("cwij,cjp->wip", kernel_own, chol, preferred_element_type=jnp.float32)
    green_part = green_part + cot_own[:, None, None] * hrot_part[None]
    d_green = lax.psum_scatter(green_part, "chol", scatter_dimension=2, tiled=True)
    green_share = lax.dynamic_slice_in_dim(greens, walk_rank * quarter, quarter, 2)
    d_chol = jnp.einsum(
        "cwji,wjp->cip", kernel_mat, green_share, preferred_element_type=jnp.float32
    )
    gbar = jnp.einsum(
        "w,wip->ip",
        energy_cot,
        greens,
        precision=lax.Precision.HIGHEST,
        preferred_element_type=jnp.float32,
    ).astype(jnp.bfloat16)
    d_trial = lax.dot_general(
        hamil, gbar, (((1,), (1,)), ((), ())), preferred_element_type=jnp.float32
    )
    return (d_green, d_chol, d_trial)


def solution(mesh):
    direct = mesh.shape["walk"] == 4 and mesh.shape["chol"] == 4
    return jax.shard_map(
        fused if direct else shards,
        mesh=mesh,
        in_specs=(
            P(("groups", "walk"), None, None),
            P(("groups", "chol"), None, None),
            P(("groups", "chol"), None),
            P("chol", None),
            P("groups"),
        ),
        out_specs=(
            P(("groups", "walk"), None, "chol"),
            P(("groups", "chol"), None, "walk"),
            P(("groups", "chol"), None),
        ),
        check_vma=False,
    )
```

```python
import functools

import jax
import jax.numpy as jnp
from jax import lax
from jax.experimental import pallas as pl
from jax.experimental.pallas import tpu as pltpu
from jax.sharding import PartitionSpec as P

MESH = pl.DeviceIdType.MESH
F32 = jnp.float32
BF16 = jnp.bfloat16
PACK = 16


def nt(a, b):
    return lax.dot_general(a, b, (((1,), (1,)), ((), ())), preferred_element_type=F32)


def nn(a, b):
    return lax.dot_general(a, b, (((1,), (0,)), ((), ())), preferred_element_type=F32)


def tn(a, b):
    return lax.dot_general(a, b, (((0,), (0,)), ((), ())), preferred_element_type=F32)


def kernel_of(exchange, cot):
    rows = lax.broadcasted_iota(jnp.int32, exchange.shape, 0)
    cols = lax.broadcasted_iota(jnp.int32, exchange.shape, 1)
    diagonal = rows == cols
    coulomb = jnp.sum(jnp.where(diagonal, exchange, 0.0))
    return (cot * (jnp.where(diagonal, coulomb, 0.0) - exchange)).astype(BF16)


def pack_tail(tail):
    rows, width = tail.shape
    full = rows // PACK * PACK
    blocks = [tail[k:k + PACK] for k in range(0, full, PACK)]
    if full < rows:
        fill = jnp.zeros((full + PACK - rows, width), tail.dtype)
        blocks.append(jnp.concatenate([tail[full:], fill], axis=0))
    return jnp.concatenate(blocks, axis=1)


def unpack_tail(packed, rows, width):
    blocks = []
    for k, start in enumerate(range(0, rows, PACK)):
        count = min(PACK, rows - start)
        blocks.append(packed[:count, k * width:(k + 1) * width])
    return jnp.concatenate(blocks, axis=0)


def put(box, index, piece):
    main = box.shape[2]
    rows, width = piece.shape
    box[index, PACK:, :] = piece[:, :main].astype(box.dtype)
    packed = pack_tail(piece[:, main:])
    box[index, :PACK, :packed.shape[1]] = packed.astype(box.dtype)


def absorb(target, index, box, slot, first, count):
    _, rows, width = target.shape
    main = box.shape[2]
    if first < PACK:
        tail = unpack_tail(box[slot, :PACK, :].astype(F32), rows, width - main)
        target[index, :, main:] += tail
    low, high = max(first, PACK), first + count
    target[index, low - PACK:high - PACK, :main] += box[slot, low:high, :].astype(F32)


def row_chunks(rows, count):
    step = -(-rows // count // 16) * 16
    starts = [k * step for k in range(count)]
    return [(s, e - s) for s, e in zip(starts, starts[1:] + [rows])]


def body(
    chunks, cot_hbm, green_hbm, chol_hbm, trial_hbm, hamil_hbm,
    dgreen_ref, dchol_ref, dtrial_ref,
    cot_ref, green_ref, chol_ref, trial_ref, hamil_ref,
    quarters, peer_quarters, kernels, peer_kernels,
    held, outbox, inbox, foldbox, chol_out, chol_in,
    part, part_in, trial_out, trial_in,
    load_sem, quarter_send, quarter_recv, kernel_send, kernel_recv,
    chol_send, chol_recv, part_send, part_recv, trial_send, trial_recv, done_send, done_recv,
    z_send, z_recv, fold_send, fold_recv, forward_send, forward_recv,
):
    n_walk, n_chol = 4, 4
    walk = lax.axis_index("walk")
    rank = lax.axis_index("chol")
    n_vec, occ, orb = chol_ref.shape
    core = walk % 2
    mate = walk + 1 - 2 * core
    across = (walk + 2) % n_walk
    quarter = orb // n_walk
    third = orb // n_chol
    half = hamil_ref.shape[0] // 2
    folds = {(0, 3): 1, (3, 0): 2}

    loads = [
        pltpu.make_async_copy(source, target, load_sem.at[k])
        for k, (source, target) in enumerate((
            (green_hbm.at[0], green_ref), (chol_hbm, chol_ref),
            (trial_hbm, trial_ref), (hamil_hbm, hamil_ref), (cot_hbm, cot_ref),
        ))
    ]
    for load in loads:
        load.start()
    barrier = pltpu.get_barrier_semaphore()
    for device in (mate, across):
        pl.semaphore_signal(barrier, inc=1, device_id={"walk": device}, device_id_type=MESH)

    def enter(r):
        @pl.when(rank == r)
        def _():
            pl.semaphore_wait(barrier, 2 + (r > 0))
            for c in (r + 1, r - 1, r - 2):
                if 0 <= c < n_chol:
                    pl.semaphore_signal(
                        barrier, inc=1, device_id={"chol": c}, device_id_type=MESH
                    )

    def remote(source, target, send, recv, axis, device):
        return pltpu.make_async_remote_copy(
            source, target, send, recv, device_id={axis: device}, device_id_type=MESH
        )

    def to_mate_quarter(k):
        index = mate if k == 0 else (mate + 2) % n_walk
        return remote(
            quarters.at[index], peer_quarters.at[k], quarter_send.at[k], quarter_recv.at[k],
            "walk", mate,
        )

    def to_mate_kernels():
        return remote(kernels, peer_kernels, kernel_send, kernel_recv, "walk", mate)

    def to_across_chol(g):
        return remote(
            chol_out.at[g], chol_in.at[g], chol_send.at[g], chol_recv.at[g], "walk", across
        )

    def rows_of(side):
        return pl.ds(pl.multiple_of(side * half, 8), half)

    def to_mate_part():
        return remote(part.at[rows_of(1 - core)], part_in, part_send, part_recv, "walk", mate)

    def to_across_trial():
        return remote(trial_out, trial_in, trial_send, trial_recv, "walk", across)

    def to_mate_done(side):
        span = rows_of(side)
        return remote(
            dtrial_ref.at[span], dtrial_ref.at[span], done_send, done_recv, "walk", mate
        )

    def to_z(r, c):
        return remote(outbox.at[c], inbox.at[r], z_send.at[c], z_recv.at[r], "chol", c)

    def to_fold(c, k, middle):
        span = pl.ds(*chunks[k])
        return remote(
            outbox.at[c, span], foldbox.at[span], fold_send.at[k], fold_recv.at[k],
            "chol", middle,
        )

    def forward(r, c, k):
        span = pl.ds(*chunks[k])
        return remote(
            outbox.at[c, span], inbox.at[r, span], forward_send.at[k], forward_recv.at[k],
            "chol", c,
        )

    def window(c):
        low = c * third // 128 * 128
        high = min(orb, -(-(c + 1) * third // 128) * 128)
        total = cot * tn(trial_ref[...], hamil_ref[:, low:high])
        for g in range(n_vec):
            total = total + nn(kernels[g], chol_ref[g, :, low:high])
        return total[:, c * third - low:(c + 1) * third - low]

    def held_at(r, c):
        return r in [middle for (_, end), middle in folds.items() if end == c]

    def copies_of(r, c):
        if (r, c) in folds:
            return [to_fold(c, k, folds[r, c]) for k in range(len(chunks))]
        if held_at(r, c):
            return [forward(r, c, k) for k in range(len(chunks))]
        return [to_z(r, c)]

    def make_piece(r, c):
        if held_at(r, c):
            put(held, 0, window(c))
        else:
            put(outbox, c, window(c))

    def start_piece(r, c):
        for copy in copies_of(r, c):
            copy.start()

    def finish_piece(r, c):
        for copy in copies_of(r, c):
            copy.wait_send()

    lines = {0: (3, 2, 1), 3: (0, 2, 1)}

    def next_piece(turn):
        for r, line in lines.items():

            @pl.when(rank == r)
            def _():
                finish_piece(r, line[turn - 1])
                start_piece(r, line[turn])

    for r in range(n_chol):
        enter(r)

    loads[0].wait()
    for q in range(n_walk):
        quarters[q] = green_ref[:, q * quarter:(q + 1) * quarter]
    loads[4].wait()
    cot = cot_ref[walk]
    loads[1].wait()
    for g in range(n_vec):
        kernels[g] = kernel_of(nt(chol_ref[g], green_ref[...]), cot)
    to_mate_quarter(1).start()
    to_mate_kernels().start()
    to_mate_quarter(0).start()
    loads[2].wait()
    loads[3].wait()

    for r, c in ((1, 0), (2, 1), (3, 0)):

        @pl.when(rank == r)
        def _():
            make_piece(r, c)
            start_piece(r, c)

    def across_chol(g):
        put(
            chol_out, g,
            tn(kernels[g], quarters[across]) + tn(peer_kernels[g], peer_quarters[1]),
        )
        to_across_chol(g).start()

    to_mate_quarter(1).wait_recv()
    to_mate_kernels().wait_recv()
    for g in range(n_vec - 1):
        across_chol(g)

    for r, order in ((0, (3, 2, 1)), (1, (2, 3)), (2, (0, 3)), (3, (2, 1))):

        @pl.when(rank == r)
        def _():
            if r < n_chol - 1:
                pl.semaphore_wait(barrier, min(2, n_chol - 1 - r))
            for c in order:
                make_piece(r, c)
                if not held_at(r, c) and (r not in lines or lines[r][0] == c):
                    start_piece(r, c)

    part[...] = cot * nt(hamil_ref[...], green_ref[...])
    to_mate_part().start()
    for r in range(n_chol):

        @pl.when(rank == r)
        def _():
            dgreen_ref[0] = window(r)

    to_mate_part().wait_recv()
    part_in[...] += part[rows_of(core), :]
    trial_out[...] = part_in[...].astype(BF16)
    to_across_trial().start()
    across_chol(n_vec - 1)
    to_mate_quarter(0).wait_recv()
    for g in range(n_vec):
        dchol_ref[g] = tn(kernels[g], quarters[walk]) + tn(peer_kernels[g], peer_quarters[0])

    next_piece(1)
    for (start, end), middle in folds.items():

        @pl.when(rank == middle)
        def _():
            for k, (first, count) in enumerate(chunks):
                span = pl.ds(first, count)
                to_fold(end, k, middle).wait_recv()
                outbox[end, span, :] = (
                    held[0, span, :] + foldbox[span, :].astype(F32)
                ).astype(BF16)
                forward(middle, end, k).start()

    def receive(r, c):
        if c in [middle for (_, end), middle in folds.items() if end == r]:
            for k, (first, count) in enumerate(chunks):
                forward(c, r, k).wait_recv()
                absorb(dgreen_ref, 0, inbox, c, first, count)
        else:
            to_z(c, r).wait_recv()
            absorb(dgreen_ref, 0, inbox, c, 0, inbox.shape[1])

    next_piece(2)
    for g in range(n_vec - 1):
        to_across_chol(g).wait_recv()
        absorb(dchol_ref, g, chol_in, g, 0, chol_in.shape[1])

    for r, c in ((0, 1), (1, 2), (2, 1), (3, 2)):

        @pl.when(rank == r)
        def _():
            receive(r, c)

    to_across_trial().wait_recv()
    dtrial_ref[rows_of(core), :] = part_in[...] + trial_in[...].astype(F32)
    to_mate_done(core).start()

    g = n_vec - 1
    to_across_chol(g).wait_recv()
    absorb(dchol_ref, g, chol_in, g, 0, chol_in.shape[1])

    for r, order in ((0, (2,)), (1, (0, 3)), (2, (3, 0)), (3, (1,))):

        @pl.when(rank == r)
        def _():
            for c in order:
                receive(r, c)

    to_mate_done(1 - core).wait_recv()

    for k in range(2):
        to_mate_quarter(k).wait_send()
    for g in range(n_vec):
        to_across_chol(g).wait_send()
    to_mate_kernels().wait_send()
    to_mate_part().wait_send()
    to_across_trial().wait_send()
    to_mate_done(core).wait_send()
    for r in range(n_chol):

        @pl.when(rank == r)
        def _():
            for c in range(n_chol):
                if c != r and (r not in lines or lines[r][-1] == c):
                    finish_piece(r, c)


def write_out(*refs):
    sources, targets, sem = refs[:3], refs[3:6], refs[6]
    copies = [pltpu.make_async_copy(s, t, sem.at[k]) for k, (s, t) in enumerate(zip(sources, targets))]
    for copy in copies:
        copy.start()
    for copy in copies:
        copy.wait()


def fused(green, chol, trial, hamil, energy_cot):
    n_chol = lax.axis_size("chol")
    n_walk = lax.axis_size("walk")
    _, occ, orb = green.shape
    n_vec = chol.shape[0]
    rows = hamil.shape[0]
    packed = (occ + PACK, orb // n_chol // 128 * 128)
    chunks = row_chunks(packed[0], 2)
    vmem = pl.BlockSpec(memory_space=pltpu.VMEM)
    anywhere = pl.BlockSpec(memory_space=pl.ANY)
    dma = pltpu.SemaphoreType.DMA
    shapes = [
        (1, occ, orb // n_chol),
        (n_vec, occ, orb // n_walk),
        (rows, occ),
    ]
    results = pl.pallas_call(
        functools.partial(body, chunks),
        out_shape=tuple(pltpu.VMEM(shape, F32) for shape in shapes),
        in_specs=[anywhere] * 5,
        out_specs=(vmem,) * 3,
        scratch_shapes=[
            pltpu.SMEM(energy_cot.shape, F32),
            pltpu.VMEM((occ, orb), BF16),
            pltpu.VMEM(chol.shape, BF16),
            pltpu.VMEM(trial.shape, BF16),
            pltpu.VMEM(hamil.shape, BF16),
            pltpu.VMEM((n_walk, occ, orb // n_walk), BF16),
            pltpu.VMEM((2, occ, orb // n_walk), BF16),
            pltpu.VMEM((n_vec, occ, occ), BF16),
            pltpu.VMEM((n_vec, occ, occ), BF16),
            pltpu.VMEM((1,) + packed, F32),
            pltpu.VMEM((n_chol,) + packed, BF16),
            pltpu.VMEM((n_chol,) + packed, BF16),
            pltpu.VMEM(packed, BF16),
            pltpu.VMEM((n_vec,) + packed, BF16),
            pltpu.VMEM((n_vec,) + packed, BF16),
            pltpu.VMEM((rows, occ), F32),
            pltpu.VMEM((rows // 2, occ), F32),
            pltpu.VMEM((rows // 2, occ), BF16),
            pltpu.VMEM((rows // 2, occ), BF16),
            dma((5,)), dma((2,)), dma((2,)), dma, dma,
            dma((n_vec,)), dma((n_vec,)), dma, dma, dma, dma, dma, dma,
            dma((n_chol,)), dma((n_chol,)),
            dma((len(chunks),)), dma((len(chunks),)), dma((len(chunks),)), dma((len(chunks),)),
        ],
        compiler_params=pltpu.CompilerParams(
            collective_id=0, has_side_effects=True, vmem_limit_bytes=60 * 1024 * 1024
        ),
    )(energy_cot, green, chol, trial, hamil)
    return pl.pallas_call(
        write_out,
        out_shape=tuple(jax.ShapeDtypeStruct(shape, F32) for shape in shapes),
        in_specs=[anywhere] * 3,
        out_specs=(anywhere,) * 3,
        scratch_shapes=[dma((3,))],
        compiler_params=pltpu.CompilerParams(vmem_limit_bytes=1024 * 1024),
    )(*results)


def shards(green, chol, trial, hamil, energy_cot):
    walk_rank = lax.axis_index("walk")
    walk_rows = green.shape[0]
    cot_own = lax.dynamic_slice_in_dim(energy_cot, walk_rank * walk_rows, walk_rows, 0)
    hrot_part = lax.dot_general(
        trial, hamil, (((0,), (0,)), ((), ())), preferred_element_type=jnp.float32
    )
    identity = jnp.eye(trial.shape[1], dtype=jnp.float32)
    quarter = green.shape[2] // lax.axis_size("walk")
    greens = lax.all_gather(green, "walk", axis=0, tiled=True)
    coulomb = jnp.einsum("cip,wip->cw", chol, greens, preferred_element_type=jnp.float32)
    exchange_mat = jnp.einsum("cip,wjp->cwij", chol, greens, preferred_element_type=jnp.float32)
    kernel_mat = (
        energy_cot[None, :, None, None] * (coulomb[:, :, None, None] * identity - exchange_mat)
    ).astype(jnp.bfloat16)
    kernel_own = lax.dynamic_slice_in_dim(kernel_mat, walk_rank * walk_rows, walk_rows, 1)
    green_part = jnp.einsum("cwij,cjp->wip", kernel_own, chol, preferred_element_type=jnp.float32)
    green_part = green_part + cot_own[:, None, None] * hrot_part[None]
    d_green = lax.psum_scatter(green_part, "chol", scatter_dimension=2, tiled=True)
    green_share = lax.dynamic_slice_in_dim(greens, walk_rank * quarter, quarter, 2)
    d_chol = jnp.einsum(
        "cwji,wjp->cip", kernel_mat, green_share, preferred_element_type=jnp.float32
    )
    gbar = jnp.einsum(
        "w,wip->ip",
        energy_cot,
        greens,
        precision=lax.Precision.HIGHEST,
        preferred_element_type=jnp.float32,
    ).astype(jnp.bfloat16)
    d_trial = lax.dot_general(
        hamil, gbar, (((1,), (1,)), ((), ())), preferred_element_type=jnp.float32
    )
    return (d_green, d_chol, d_trial)


def solution(mesh):
    direct = mesh.shape["walk"] == 4 and mesh.shape["chol"] == 4
    return jax.shard_map(
        fused if direct else shards,
        mesh=mesh,
        in_specs=(
            P(("groups", "walk"), None, None),
            P(("groups", "chol"), None, None),
            P(("groups", "chol"), None),
            P("chol", None),
            P("groups"),
        ),
        out_specs=(
            P(("groups", "walk"), None, "chol"),
            P(("groups", "chol"), None, "walk"),
            P(("groups", "chol"), None),
        ),
        check_vma=False,
    )
```

```python
import functools

import jax
import jax.numpy as jnp
from jax import lax
from jax.experimental import pallas as pl
from jax.experimental.pallas import tpu as pltpu
from jax.sharding import PartitionSpec as P

MESH = pl.DeviceIdType.MESH
F32 = jnp.float32
BF16 = jnp.bfloat16
PACK = 16


def nt(a, b):
    return lax.dot_general(a, b, (((1,), (1,)), ((), ())), preferred_element_type=F32)


def nn(a, b):
    return lax.dot_general(a, b, (((1,), (0,)), ((), ())), preferred_element_type=F32)


def tn(a, b):
    return lax.dot_general(a, b, (((0,), (0,)), ((), ())), preferred_element_type=F32)


def kernel_of(exchange, cot):
    rows = lax.broadcasted_iota(jnp.int32, exchange.shape, 0)
    cols = lax.broadcasted_iota(jnp.int32, exchange.shape, 1)
    diagonal = rows == cols
    coulomb = jnp.sum(jnp.where(diagonal, exchange, 0.0))
    return (cot * (jnp.where(diagonal, coulomb, 0.0) - exchange)).astype(BF16)


def pack_tail(tail):
    rows, width = tail.shape
    full = rows // PACK * PACK
    blocks = [tail[k:k + PACK] for k in range(0, full, PACK)]
    if full < rows:
        fill = jnp.zeros((full + PACK - rows, width), tail.dtype)
        blocks.append(jnp.concatenate([tail[full:], fill], axis=0))
    return jnp.concatenate(blocks, axis=1)


def unpack_tail(packed, rows, width):
    blocks = []
    for k, start in enumerate(range(0, rows, PACK)):
        count = min(PACK, rows - start)
        blocks.append(packed[:count, k * width:(k + 1) * width])
    return jnp.concatenate(blocks, axis=0)


def put(box, index, piece):
    main = box.shape[2]
    rows, width = piece.shape
    box[index, PACK:, :] = piece[:, :main].astype(box.dtype)
    packed = pack_tail(piece[:, main:])
    box[index, :PACK, :packed.shape[1]] = packed.astype(box.dtype)


def absorb(target, index, box, slot, first, count):
    _, rows, width = target.shape
    main = box.shape[2]
    if first < PACK:
        tail = unpack_tail(box[slot, :PACK, :].astype(F32), rows, width - main)
        target[index, :, main:] += tail
    low, high = max(first, PACK), first + count
    target[index, low - PACK:high - PACK, :main] += box[slot, low:high, :].astype(F32)


def row_chunks(rows, count):
    step = -(-rows // count // 16) * 16
    starts = [k * step for k in range(count)]
    return [(s, e - s) for s, e in zip(starts, starts[1:] + [rows])]


def body(
    chunks, cot_hbm, green_hbm, chol_hbm, trial_hbm, hamil_hbm,
    dgreen_ref, dchol_ref, dtrial_ref,
    cot_ref, green_ref, chol_ref, trial_ref, hamil_ref,
    quarters, peer_quarters, kernels, peer_kernels,
    held, outbox, inbox, foldbox, chol_out, chol_in,
    part, part_in, trial_out, trial_in,
    load_sem, quarter_send, quarter_recv, kernel_send, kernel_recv,
    chol_send, chol_recv, part_send, part_recv, trial_send, trial_recv, done_send, done_recv,
    z_send, z_recv, fold_send, fold_recv, near, far,
):
    n_walk, n_chol = 4, 4
    walk = lax.axis_index("walk")
    rank = lax.axis_index("chol")
    n_vec, occ, orb = chol_ref.shape
    core = walk % 2
    mate = walk + 1 - 2 * core
    across = (walk + 2) % n_walk
    quarter = orb // n_walk
    third = orb // n_chol
    half = hamil_ref.shape[0] // 2
    folds = {(0, 3): 1, (3, 0): 2}

    loads = [
        pltpu.make_async_copy(source, target, load_sem.at[k])
        for k, (source, target) in enumerate((
            (green_hbm.at[0], green_ref), (chol_hbm, chol_ref),
            (trial_hbm, trial_ref), (hamil_hbm, hamil_ref), (cot_hbm, cot_ref),
        ))
    ]
    for load in loads:
        load.start()
    barrier = pltpu.get_barrier_semaphore()
    for device in (mate, across):
        pl.semaphore_signal(barrier, inc=1, device_id={"walk": device}, device_id_type=MESH)

    def enter(r):
        @pl.when(rank == r)
        def _():
            pl.semaphore_wait(barrier, 2 + (r > 0))
            for c, entered in ((r + 1, barrier), (r - 1, near), (r - 2, far)):
                if 0 <= c < n_chol:
                    pl.semaphore_signal(
                        entered, inc=1, device_id={"chol": c}, device_id_type=MESH
                    )

    def remote(source, target, send, recv, axis, device):
        return pltpu.make_async_remote_copy(
            source, target, send, recv, device_id={axis: device}, device_id_type=MESH
        )

    def to_mate_quarter(k):
        index = mate if k == 0 else (mate + 2) % n_walk
        return remote(
            quarters.at[index], peer_quarters.at[k], quarter_send.at[k], quarter_recv.at[k],
            "walk", mate,
        )

    def to_mate_kernels():
        return remote(kernels, peer_kernels, kernel_send, kernel_recv, "walk", mate)

    def to_across_chol(g):
        return remote(
            chol_out.at[g], chol_in.at[g], chol_send.at[g], chol_recv.at[g], "walk", across
        )

    def rows_of(side):
        return pl.ds(pl.multiple_of(side * half, 8), half)

    def to_mate_part():
        return remote(part.at[rows_of(1 - core)], part_in, part_send, part_recv, "walk", mate)

    def to_across_trial():
        return remote(trial_out, trial_in, trial_send, trial_recv, "walk", across)

    def to_mate_done(side):
        span = rows_of(side)
        return remote(
            dtrial_ref.at[span], dtrial_ref.at[span], done_send, done_recv, "walk", mate
        )

    def to_z(r, c, k):
        span = pl.ds(*chunks[k])
        return remote(
            outbox.at[c, span], inbox.at[r, span], z_send.at[c, k], z_recv.at[r, k], "chol", c
        )

    def to_fold(c, k, middle):
        span = pl.ds(*chunks[k])
        return remote(
            outbox.at[c, span], foldbox.at[span], fold_send.at[k], fold_recv.at[k],
            "chol", middle,
        )

    def window(c):
        low = c * third // 128 * 128
        high = min(orb, -(-(c + 1) * third // 128) * 128)
        total = cot * tn(trial_ref[...], hamil_ref[:, low:high])
        for g in range(n_vec):
            total = total + nn(kernels[g], chol_ref[g, :, low:high])
        return total[:, c * third - low:(c + 1) * third - low]

    def held_at(r, c):
        return r in [middle for (_, end), middle in folds.items() if end == c]

    def piece_part(r, c, k):
        if (r, c) in folds:
            return to_fold(c, k, folds[r, c])
        return to_z(r, c, k)

    def make_piece(r, c):
        if held_at(r, c):
            put(held, 0, window(c))
        else:
            put(outbox, c, window(c))

    def start_piece(r, c):
        for k in range(len(chunks)):
            piece_part(r, c, k).start()

    lines = {0: (3, 1, 2), 3: (0, 2, 1)}

    def next_piece(turn):
        for r, line in lines.items():

            @pl.when(rank == r)
            def _():
                piece_part(r, line[turn - 1], 0).wait_send()
                start_piece(r, line[turn])

    for r in range(n_chol):
        enter(r)

    loads[0].wait()
    for q in range(n_walk):
        quarters[q] = green_ref[:, q * quarter:(q + 1) * quarter]
    to_mate_quarter(1).start()
    to_mate_quarter(0).start()
    loads[4].wait()
    cot = cot_ref[walk]
    loads[1].wait()
    for g in range(n_vec):
        kernels[g] = kernel_of(nt(chol_ref[g], green_ref[...]), cot)
    to_mate_kernels().start()
    loads[2].wait()
    loads[3].wait()

    for r, c in ((0, 3), (1, 0), (2, 1), (3, 0)):

        @pl.when(rank == r)
        def _():
            make_piece(r, c)
            if r == 0:
                pl.semaphore_wait(near, 1)
            start_piece(r, c)

    part[...] = cot * nt(hamil_ref[...], green_ref[...])
    to_mate_part().start()

    for r, c in ((0, lines[0][1]), (1, 2), (2, 3), (3, lines[3][1])):

        @pl.when(rank == r)
        def _():
            make_piece(r, c)
            if r not in lines:
                pl.semaphore_wait(near, 1)
                start_piece(r, c)

    def across_chol(g):
        put(
            chol_out, g,
            tn(kernels[g], quarters[across]) + tn(peer_kernels[g], peer_quarters[1]),
        )
        to_across_chol(g).start()

    to_mate_quarter(1).wait_recv()
    to_mate_kernels().wait_recv()
    for g in range(n_vec - 1):
        across_chol(g)
    to_mate_part().wait_recv()
    part_in[...] += part[rows_of(core), :]
    trial_out[...] = part_in[...].astype(BF16)
    to_across_trial().start()
    across_chol(n_vec - 1)

    for r, c in ((0, lines[0][2]), (1, 3), (2, 0), (3, lines[3][2])):

        @pl.when(rank == r)
        def _():
            make_piece(r, c)
            if r < 2:
                pl.semaphore_wait(far, 1)

    next_piece(1)
    for (start, end), middle in folds.items():

        @pl.when(rank == middle)
        def _():
            for k, (first, count) in enumerate(chunks):
                span = pl.ds(first, count)
                to_fold(end, k, middle).wait_recv()
                outbox[end, span, :] = (
                    held[0, span, :] + foldbox[span, :].astype(F32)
                ).astype(BF16)
                to_z(middle, end, k).start()

    def receive(r, c):
        for k, (first, count) in enumerate(chunks):
            to_z(c, r, k).wait_recv()
            absorb(dgreen_ref, 0, inbox, c, first, count)

    for r in range(n_chol):

        @pl.when(rank == r)
        def _():
            dgreen_ref[0] = window(r)

    to_mate_quarter(0).wait_recv()
    for g in range(n_vec):
        dchol_ref[g] = tn(kernels[g], quarters[walk]) + tn(peer_kernels[g], peer_quarters[0])

    next_piece(2)
    for g in range(n_vec - 1):
        to_across_chol(g).wait_recv()
        absorb(dchol_ref, g, chol_in, g, 0, chol_in.shape[1])

    for r, c in ((0, 1), (1, 2), (2, 1), (3, 2)):

        @pl.when(rank == r)
        def _():
            receive(r, c)

    to_across_trial().wait_recv()
    dtrial_ref[rows_of(core), :] = part_in[...] + trial_in[...].astype(F32)
    to_mate_done(core).start()

    g = n_vec - 1
    to_across_chol(g).wait_recv()
    absorb(dchol_ref, g, chol_in, g, 0, chol_in.shape[1])

    for r, order in ((0, (2,)), (1, (0, 3)), (2, (3, 0)), (3, (1,))):

        @pl.when(rank == r)
        def _():
            for c in order:
                receive(r, c)

    to_mate_done(1 - core).wait_recv()

    for k in range(2):
        to_mate_quarter(k).wait_send()
    for g in range(n_vec):
        to_across_chol(g).wait_send()
    to_mate_kernels().wait_send()
    to_mate_part().wait_send()
    to_across_trial().wait_send()
    to_mate_done(core).wait_send()
    for r in range(n_chol):

        @pl.when(rank == r)
        def _():
            for c in range(n_chol):
                for k in range(len(chunks)):
                    if c != r and (r not in lines or k > 0 or lines[r][-1] == c):
                        piece_part(r, c, k).wait_send()


def write_out(*refs):
    sources, targets, sem = refs[:3], refs[3:6], refs[6]
    copies = [pltpu.make_async_copy(s, t, sem.at[k]) for k, (s, t) in enumerate(zip(sources, targets))]
    for copy in copies:
        copy.start()
    for copy in copies:
        copy.wait()


def fused(green, chol, trial, hamil, energy_cot):
    n_chol = lax.axis_size("chol")
    n_walk = lax.axis_size("walk")
    _, occ, orb = green.shape
    n_vec = chol.shape[0]
    rows = hamil.shape[0]
    packed = (occ + PACK, orb // n_chol // 128 * 128)
    chunks = row_chunks(packed[0], 2)
    vmem = pl.BlockSpec(memory_space=pltpu.VMEM)
    anywhere = pl.BlockSpec(memory_space=pl.ANY)
    dma = pltpu.SemaphoreType.DMA
    shapes = [
        (1, occ, orb // n_chol),
        (n_vec, occ, orb // n_walk),
        (rows, occ),
    ]
    results = pl.pallas_call(
        functools.partial(body, chunks),
        out_shape=tuple(pltpu.VMEM(shape, F32) for shape in shapes),
        in_specs=[anywhere] * 5,
        out_specs=(vmem,) * 3,
        scratch_shapes=[
            pltpu.SMEM(energy_cot.shape, F32),
            pltpu.VMEM((occ, orb), BF16),
            pltpu.VMEM(chol.shape, BF16),
            pltpu.VMEM(trial.shape, BF16),
            pltpu.VMEM(hamil.shape, BF16),
            pltpu.VMEM((n_walk, occ, orb // n_walk), BF16),
            pltpu.VMEM((2, occ, orb // n_walk), BF16),
            pltpu.VMEM((n_vec, occ, occ), BF16),
            pltpu.VMEM((n_vec, occ, occ), BF16),
            pltpu.VMEM((1,) + packed, F32),
            pltpu.VMEM((n_chol,) + packed, BF16),
            pltpu.VMEM((n_chol,) + packed, BF16),
            pltpu.VMEM(packed, BF16),
            pltpu.VMEM((n_vec,) + packed, BF16),
            pltpu.VMEM((n_vec,) + packed, BF16),
            pltpu.VMEM((rows, occ), F32),
            pltpu.VMEM((rows // 2, occ), F32),
            pltpu.VMEM((rows // 2, occ), BF16),
            pltpu.VMEM((rows // 2, occ), BF16),
            dma((5,)), dma((2,)), dma((2,)), dma, dma,
            dma((n_vec,)), dma((n_vec,)), dma, dma, dma, dma, dma, dma,
            dma((n_chol, len(chunks))), dma((n_chol, len(chunks))),
            dma((len(chunks),)), dma((len(chunks),)),
            pltpu.SemaphoreType.REGULAR, pltpu.SemaphoreType.REGULAR,
        ],
        compiler_params=pltpu.CompilerParams(
            collective_id=0, has_side_effects=True, vmem_limit_bytes=60 * 1024 * 1024
        ),
    )(energy_cot, green, chol, trial, hamil)
    return pl.pallas_call(
        write_out,
        out_shape=tuple(jax.ShapeDtypeStruct(shape, F32) for shape in shapes),
        in_specs=[anywhere] * 3,
        out_specs=(anywhere,) * 3,
        scratch_shapes=[dma((3,))],
        compiler_params=pltpu.CompilerParams(vmem_limit_bytes=1024 * 1024),
    )(*results)


def shards(green, chol, trial, hamil, energy_cot):
    walk_rank = lax.axis_index("walk")
    walk_rows = green.shape[0]
    cot_own = lax.dynamic_slice_in_dim(energy_cot, walk_rank * walk_rows, walk_rows, 0)
    hrot_part = lax.dot_general(
        trial, hamil, (((0,), (0,)), ((), ())), preferred_element_type=jnp.float32
    )
    identity = jnp.eye(trial.shape[1], dtype=jnp.float32)
    quarter = green.shape[2] // lax.axis_size("walk")
    greens = lax.all_gather(green, "walk", axis=0, tiled=True)
    coulomb = jnp.einsum("cip,wip->cw", chol, greens, preferred_element_type=jnp.float32)
    exchange_mat = jnp.einsum("cip,wjp->cwij", chol, greens, preferred_element_type=jnp.float32)
    kernel_mat = (
        energy_cot[None, :, None, None] * (coulomb[:, :, None, None] * identity - exchange_mat)
    ).astype(jnp.bfloat16)
    kernel_own = lax.dynamic_slice_in_dim(kernel_mat, walk_rank * walk_rows, walk_rows, 1)
    green_part = jnp.einsum("cwij,cjp->wip", kernel_own, chol, preferred_element_type=jnp.float32)
    green_part = green_part + cot_own[:, None, None] * hrot_part[None]
    d_green = lax.psum_scatter(green_part, "chol", scatter_dimension=2, tiled=True)
    green_share = lax.dynamic_slice_in_dim(greens, walk_rank * quarter, quarter, 2)
    d_chol = jnp.einsum(
        "cwji,wjp->cip", kernel_mat, green_share, preferred_element_type=jnp.float32
    )
    gbar = jnp.einsum(
        "w,wip->ip",
        energy_cot,
        greens,
        precision=lax.Precision.HIGHEST,
        preferred_element_type=jnp.float32,
    ).astype(jnp.bfloat16)
    d_trial = lax.dot_general(
        hamil, gbar, (((1,), (1,)), ((), ())), preferred_element_type=jnp.float32
    )
    return (d_green, d_chol, d_trial)


def solution(mesh):
    direct = mesh.shape["walk"] == 4 and mesh.shape["chol"] == 4
    return jax.shard_map(
        fused if direct else shards,
        mesh=mesh,
        in_specs=(
            P(("groups", "walk"), None, None),
            P(("groups", "chol"), None, None),
            P(("groups", "chol"), None),
            P("chol", None),
            P("groups"),
        ),
        out_specs=(
            P(("groups", "walk"), None, "chol"),
            P(("groups", "chol"), None, "walk"),
            P(("groups", "chol"), None),
        ),
        check_vma=False,
    )
```

```python
import functools

import jax
import jax.numpy as jnp
from jax import lax
from jax.experimental import pallas as pl
from jax.experimental.pallas import tpu as pltpu
from jax.sharding import PartitionSpec as P

MESH = pl.DeviceIdType.MESH
F32 = jnp.float32
BF16 = jnp.bfloat16
PACK = 16
LANE = 128
TRIAL = 128


def nt(a, b):
    return lax.dot_general(a, b, (((1,), (1,)), ((), ())), preferred_element_type=F32)


def nn(a, b):
    return lax.dot_general(a, b, (((1,), (0,)), ((), ())), preferred_element_type=F32)


def tn(a, b):
    return lax.dot_general(a, b, (((0,), (0,)), ((), ())), preferred_element_type=F32)


def kernel_of(exchange, cot):
    rows = lax.broadcasted_iota(jnp.int32, exchange.shape, 0)
    cols = lax.broadcasted_iota(jnp.int32, exchange.shape, 1)
    diagonal = rows == cols
    coulomb = jnp.sum(jnp.where(diagonal, exchange, 0.0))
    return (cot * (jnp.where(diagonal, coulomb, 0.0) - exchange)).astype(BF16)


def pack_tail(tail):
    rows, width = tail.shape
    full = rows // PACK * PACK
    blocks = [tail[k:k + PACK] for k in range(0, full, PACK)]
    if full < rows:
        fill = jnp.zeros((full + PACK - rows, width), tail.dtype)
        blocks.append(jnp.concatenate([tail[full:], fill], axis=0))
    return jnp.concatenate(blocks, axis=1)


def unpack_tail(packed, rows, width):
    blocks = []
    for k, start in enumerate(range(0, rows, PACK)):
        count = min(PACK, rows - start)
        blocks.append(packed[:count, k * width:(k + 1) * width])
    return jnp.concatenate(blocks, axis=0)


def put(box, index, piece):
    main = box.shape[2]
    rows, width = piece.shape
    box[index, PACK:, :] = piece[:, :main].astype(box.dtype)
    packed = pack_tail(piece[:, main:])
    box[index, :PACK, :packed.shape[1]] = packed.astype(box.dtype)


def put_trial(box, value):
    rows, lanes = value.shape
    box[TRIAL:, :] = value[:, :LANE].astype(box.dtype)
    middle = value[:, LANE:LANE + LANE // 2].astype(box.dtype)
    split = TRIAL - PACK
    box[PACK:TRIAL, :LANE // 2] = middle[:split]
    box[PACK:PACK + rows - split, LANE // 2:] = middle[split:]
    packed = pack_tail(value[:, LANE + LANE // 2:])
    box[:PACK, :packed.shape[1]] = packed.astype(box.dtype)


def rest_of_trial(box, rows, lanes):
    split = TRIAL - PACK
    pair = box[PACK:TRIAL, :].astype(F32)
    middle = jnp.concatenate(
        [pair[:, :LANE // 2], pair[:rows - split, LANE // 2:]], axis=0
    )
    tail = unpack_tail(box[:PACK, :].astype(F32), rows, lanes - LANE - LANE // 2)
    return jnp.concatenate([middle, tail], axis=1)


def absorb(target, index, box, slot, first, count):
    _, rows, width = target.shape
    main = box.shape[2]
    if first < PACK:
        tail = unpack_tail(box[slot, :PACK, :].astype(F32), rows, width - main)
        target[index, :, main:] += tail
    low, high = max(first, PACK), first + count
    target[index, low - PACK:high - PACK, :main] += box[slot, low:high, :].astype(F32)


def row_chunks(rows, count):
    step = -(-rows // count // 16) * 16
    starts = [k * step for k in range(count)]
    return [(s, e - s) for s, e in zip(starts, starts[1:] + [rows])]


def body(
    chunks, cot_hbm, green_hbm, chol_hbm, trial_hbm, hamil_hbm,
    dgreen_ref, dchol_ref, dtrial_ref,
    cot_ref, green_ref, chol_ref, trial_ref, hamil_ref,
    quarters, peer_quarters, kernels, peer_kernels,
    held, outbox, inbox, foldbox, chol_out, chol_in,
    part, part_in, trial_out, trial_in,
    load_sem, quarter_send, quarter_recv, kernel_send, kernel_recv,
    chol_send, chol_recv, part_send, part_recv, trial_send, trial_recv, done_send, done_recv,
    z_send, z_recv, fold_send, fold_recv, near, far,
):
    n_walk, n_chol = 4, 4
    walk = lax.axis_index("walk")
    rank = lax.axis_index("chol")
    n_vec, occ, orb = chol_ref.shape
    core = walk % 2
    mate = walk + 1 - 2 * core
    across = (walk + 2) % n_walk
    quarter = orb // n_walk
    third = orb // n_chol
    half = hamil_ref.shape[0] // 2
    folds = {(0, 3): 1, (3, 0): 2}

    loads = [
        pltpu.make_async_copy(source, target, load_sem.at[k])
        for k, (source, target) in enumerate((
            (green_hbm.at[0], green_ref), (chol_hbm, chol_ref),
            (trial_hbm, trial_ref), (hamil_hbm, hamil_ref), (cot_hbm, cot_ref),
        ))
    ]
    for load in loads:
        load.start()
    barrier = pltpu.get_barrier_semaphore()
    for device in (mate, across):
        pl.semaphore_signal(barrier, inc=1, device_id={"walk": device}, device_id_type=MESH)

    def enter(r):
        @pl.when(rank == r)
        def _():
            pl.semaphore_wait(barrier, 2 + (r > 0))
            for c, entered in ((r + 1, barrier), (r - 1, near), (r - 2, far)):
                if 0 <= c < n_chol:
                    pl.semaphore_signal(
                        entered, inc=1, device_id={"chol": c}, device_id_type=MESH
                    )

    def remote(source, target, send, recv, axis, device):
        return pltpu.make_async_remote_copy(
            source, target, send, recv, device_id={axis: device}, device_id_type=MESH
        )

    def to_mate_quarter(k):
        index = mate if k == 0 else (mate + 2) % n_walk
        return remote(
            quarters.at[index], peer_quarters.at[k], quarter_send.at[k], quarter_recv.at[k],
            "walk", mate,
        )

    def to_mate_kernels():
        return remote(kernels, peer_kernels, kernel_send, kernel_recv, "walk", mate)

    def to_across_chol(g):
        return remote(
            chol_out.at[g], chol_in.at[g], chol_send.at[g], chol_recv.at[g], "walk", across
        )

    def rows_of(side):
        return pl.ds(pl.multiple_of(side * half, 8), half)

    def to_mate_part():
        return remote(part.at[rows_of(1 - core)], part_in, part_send, part_recv, "walk", mate)

    def to_across_trial():
        return remote(trial_out, trial_in, trial_send, trial_recv, "walk", across)

    def to_mate_done(side):
        span = rows_of(side)
        return remote(
            dtrial_ref.at[span], dtrial_ref.at[span], done_send, done_recv, "walk", mate
        )

    def to_z(r, c, k):
        span = pl.ds(*chunks[k])
        return remote(
            outbox.at[c, span], inbox.at[r, span], z_send.at[c, k], z_recv.at[r, k], "chol", c
        )

    def to_fold(c, k, middle):
        span = pl.ds(*chunks[k])
        return remote(
            outbox.at[c, span], foldbox.at[span], fold_send.at[k], fold_recv.at[k],
            "chol", middle,
        )

    def window(c):
        low = c * third // 128 * 128
        high = min(orb, -(-(c + 1) * third // 128) * 128)
        total = cot * tn(trial_ref[...], hamil_ref[:, low:high])
        for g in range(n_vec):
            total = total + nn(kernels[g], chol_ref[g, :, low:high])
        return total[:, c * third - low:(c + 1) * third - low]

    def held_at(r, c):
        return r in [middle for (_, end), middle in folds.items() if end == c]

    def piece_part(r, c, k):
        if (r, c) in folds:
            return to_fold(c, k, folds[r, c])
        return to_z(r, c, k)

    def make_piece(r, c):
        if held_at(r, c):
            put(held, 0, window(c))
        else:
            put(outbox, c, window(c))

    def start_piece(r, c):
        for k in range(len(chunks)):
            piece_part(r, c, k).start()

    lines = {0: (3, 1, 2), 3: (0, 2, 1)}

    def next_piece(r, turn):
        piece_part(r, lines[r][turn - 1], 0).wait_send()
        start_piece(r, lines[r][turn])

    for r in range(n_chol - 1):
        enter(r)

    loads[0].wait()
    for q in range(n_walk):
        quarters[q] = green_ref[:, q * quarter:(q + 1) * quarter]
    loads[4].wait()
    cot = cot_ref[walk]
    loads[1].wait()
    for g in range(n_vec):
        kernels[g] = kernel_of(nt(chol_ref[g], green_ref[...]), cot)
    enter(n_chol - 1)
    to_mate_quarter(1).start()
    to_mate_kernels().start()
    to_mate_quarter(0).start()
    loads[2].wait()
    loads[3].wait()

    for r, c in ((0, 3), (1, 0), (2, 1), (3, 0)):

        @pl.when(rank == r)
        def _():
            make_piece(r, c)
            if r == 0:
                pl.semaphore_wait(near, 1)
            start_piece(r, c)

    part[...] = cot * nt(hamil_ref[...], green_ref[...])
    to_mate_part().start()

    for r, c in ((1, 2), (2, 3), (3, lines[3][1])):

        @pl.when(rank == r)
        def _():
            make_piece(r, c)
            if r not in lines:
                pl.semaphore_wait(near, 1)
                start_piece(r, c)

    def across_chol(g):
        put(
            chol_out, g,
            tn(kernels[g], quarters[across]) + tn(peer_kernels[g], peer_quarters[1]),
        )
        to_across_chol(g).start()

    to_mate_quarter(1).wait_recv()
    to_mate_kernels().wait_recv()
    for g in range(n_vec - 1):
        across_chol(g)

    to_mate_part().wait_recv()
    part_in[...] += part[rows_of(core), :]
    put_trial(trial_out, part_in[...])
    to_across_trial().start()
    across_chol(n_vec - 1)

    for r, order in ((0, lines[0][1:]), (1, (3,)), (2, (0,)), (3, lines[3][2:])):

        @pl.when(rank == r)
        def _():
            for k, c in enumerate(order):
                make_piece(r, c)
                if r == 0 and k == 0:
                    next_piece(r, 1)
            if r < 2:
                pl.semaphore_wait(far, 1)
            if r == 3:
                next_piece(r, 1)

    for (start, end), middle in folds.items():

        @pl.when(rank == middle)
        def _():
            for k, (first, count) in enumerate(chunks):
                span = pl.ds(first, count)
                to_fold(end, k, middle).wait_recv()
                outbox[end, span, :] = (
                    held[0, span, :] + foldbox[span, :].astype(F32)
                ).astype(BF16)
                to_z(middle, end, k).start()

    def receive(r, c):
        for k, (first, count) in enumerate(chunks):
            to_z(c, r, k).wait_recv()
            absorb(dgreen_ref, 0, inbox, c, first, count)

    for r in range(n_chol):

        @pl.when(rank == r)
        def _():
            dgreen_ref[0] = window(r)

    to_mate_quarter(0).wait_recv()
    for g in range(n_vec):
        dchol_ref[g] = tn(kernels[g], quarters[walk]) + tn(peer_kernels[g], peer_quarters[0])

    for r in lines:

        @pl.when(rank == r)
        def _():
            next_piece(r, 2)

    for g in range(n_vec - 1):
        to_across_chol(g).wait_recv()
        absorb(dchol_ref, g, chol_in, g, 0, chol_in.shape[1])

    for r, c in ((0, 1), (1, 2), (2, 1), (3, 2)):

        @pl.when(rank == r)
        def _():
            receive(r, c)

    to_across_trial().wait_recv()
    span = rows_of(core)
    half_rows = trial_in[TRIAL:, :].astype(F32)
    dtrial_ref[span, :LANE] = part_in[:, :LANE] + half_rows
    dtrial_ref[span, LANE:] = part_in[:, LANE:] + rest_of_trial(trial_in, half, occ)
    to_mate_done(core).start()

    g = n_vec - 1
    to_across_chol(g).wait_recv()
    absorb(dchol_ref, g, chol_in, g, 0, chol_in.shape[1])

    for r, order in ((0, (2,)), (1, (0, 3)), (2, (3, 0)), (3, (1,))):

        @pl.when(rank == r)
        def _():
            for c in order:
                receive(r, c)

    to_mate_done(1 - core).wait_recv()

    for k in range(2):
        to_mate_quarter(k).wait_send()
    for g in range(n_vec):
        to_across_chol(g).wait_send()
    to_mate_kernels().wait_send()
    to_mate_part().wait_send()
    to_across_trial().wait_send()
    to_mate_done(core).wait_send()
    for r in range(n_chol):

        @pl.when(rank == r)
        def _():
            for c in range(n_chol):
                for k in range(len(chunks)):
                    if c != r and (r not in lines or k > 0 or lines[r][-1] == c):
                        piece_part(r, c, k).wait_send()


def write_out(*refs):
    sources, targets, sem = refs[:3], refs[3:6], refs[6]
    copies = [pltpu.make_async_copy(s, t, sem.at[k]) for k, (s, t) in enumerate(zip(sources, targets))]
    for copy in copies:
        copy.start()
    for copy in copies:
        copy.wait()


def fused(green, chol, trial, hamil, energy_cot):
    n_chol = lax.axis_size("chol")
    n_walk = lax.axis_size("walk")
    _, occ, orb = green.shape
    n_vec = chol.shape[0]
    rows = hamil.shape[0]
    packed = (occ + PACK, orb // n_chol // 128 * 128)
    chunks = row_chunks(packed[0], 2)
    vmem = pl.BlockSpec(memory_space=pltpu.VMEM)
    anywhere = pl.BlockSpec(memory_space=pl.ANY)
    dma = pltpu.SemaphoreType.DMA
    shapes = [
        (1, occ, orb // n_chol),
        (n_vec, occ, orb // n_walk),
        (rows, occ),
    ]
    results = pl.pallas_call(
        functools.partial(body, chunks),
        out_shape=tuple(pltpu.VMEM(shape, F32) for shape in shapes),
        in_specs=[anywhere] * 5,
        out_specs=(vmem,) * 3,
        scratch_shapes=[
            pltpu.SMEM(energy_cot.shape, F32),
            pltpu.VMEM((occ, orb), BF16),
            pltpu.VMEM(chol.shape, BF16),
            pltpu.VMEM(trial.shape, BF16),
            pltpu.VMEM(hamil.shape, BF16),
            pltpu.VMEM((n_walk, occ, orb // n_walk), BF16),
            pltpu.VMEM((2, occ, orb // n_walk), BF16),
            pltpu.VMEM((n_vec, occ, occ), BF16),
            pltpu.VMEM((n_vec, occ, occ), BF16),
            pltpu.VMEM((1,) + packed, F32),
            pltpu.VMEM((n_chol,) + packed, BF16),
            pltpu.VMEM((n_chol,) + packed, BF16),
            pltpu.VMEM(packed, BF16),
            pltpu.VMEM((n_vec,) + packed, BF16),
            pltpu.VMEM((n_vec,) + packed, BF16),
            pltpu.VMEM((rows, occ), F32),
            pltpu.VMEM((rows // 2, occ), F32),
            pltpu.VMEM((rows // 2 + TRIAL, LANE), BF16),
            pltpu.VMEM((rows // 2 + TRIAL, LANE), BF16),
            dma((5,)), dma((2,)), dma((2,)), dma, dma,
            dma((n_vec,)), dma((n_vec,)), dma, dma, dma, dma, dma, dma,
            dma((n_chol, len(chunks))), dma((n_chol, len(chunks))),
            dma((len(chunks),)), dma((len(chunks),)),
            pltpu.SemaphoreType.REGULAR, pltpu.SemaphoreType.REGULAR,
        ],
        compiler_params=pltpu.CompilerParams(
            collective_id=0, has_side_effects=True, vmem_limit_bytes=60 * 1024 * 1024
        ),
    )(energy_cot, green, chol, trial, hamil)
    return pl.pallas_call(
        write_out,
        out_shape=tuple(jax.ShapeDtypeStruct(shape, F32) for shape in shapes),
        in_specs=[anywhere] * 3,
        out_specs=(anywhere,) * 3,
        scratch_shapes=[dma((3,))],
        compiler_params=pltpu.CompilerParams(vmem_limit_bytes=1024 * 1024),
    )(*results)


def shards(green, chol, trial, hamil, energy_cot):
    walk_rank = lax.axis_index("walk")
    walk_rows = green.shape[0]
    cot_own = lax.dynamic_slice_in_dim(energy_cot, walk_rank * walk_rows, walk_rows, 0)
    hrot_part = lax.dot_general(
        trial, hamil, (((0,), (0,)), ((), ())), preferred_element_type=jnp.float32
    )
    identity = jnp.eye(trial.shape[1], dtype=jnp.float32)
    quarter = green.shape[2] // lax.axis_size("walk")
    greens = lax.all_gather(green, "walk", axis=0, tiled=True)
    coulomb = jnp.einsum("cip,wip->cw", chol, greens, preferred_element_type=jnp.float32)
    exchange_mat = jnp.einsum("cip,wjp->cwij", chol, greens, preferred_element_type=jnp.float32)
    kernel_mat = (
        energy_cot[None, :, None, None] * (coulomb[:, :, None, None] * identity - exchange_mat)
    ).astype(jnp.bfloat16)
    kernel_own = lax.dynamic_slice_in_dim(kernel_mat, walk_rank * walk_rows, walk_rows, 1)
    green_part = jnp.einsum("cwij,cjp->wip", kernel_own, chol, preferred_element_type=jnp.float32)
    green_part = green_part + cot_own[:, None, None] * hrot_part[None]
    d_green = lax.psum_scatter(green_part, "chol", scatter_dimension=2, tiled=True)
    green_share = lax.dynamic_slice_in_dim(greens, walk_rank * quarter, quarter, 2)
    d_chol = jnp.einsum(
        "cwji,wjp->cip", kernel_mat, green_share, preferred_element_type=jnp.float32
    )
    gbar = jnp.einsum(
        "w,wip->ip",
        energy_cot,
        greens,
        precision=lax.Precision.HIGHEST,
        preferred_element_type=jnp.float32,
    ).astype(jnp.bfloat16)
    d_trial = lax.dot_general(
        hamil, gbar, (((1,), (1,)), ((), ())), preferred_element_type=jnp.float32
    )
    return (d_green, d_chol, d_trial)


def solution(mesh):
    direct = mesh.shape["walk"] == 4 and mesh.shape["chol"] == 4
    return jax.shard_map(
        fused if direct else shards,
        mesh=mesh,
        in_specs=(
            P(("groups", "walk"), None, None),
            P(("groups", "chol"), None, None),
            P(("groups", "chol"), None),
            P("chol", None),
            P("groups"),
        ),
        out_specs=(
            P(("groups", "walk"), None, "chol"),
            P(("groups", "chol"), None, "walk"),
            P(("groups", "chol"), None),
        ),
        check_vma=False,
    )
```

```python
import functools

import jax
import jax.numpy as jnp
from jax import lax
from jax.experimental import pallas as pl
from jax.experimental.pallas import tpu as pltpu
from jax.sharding import PartitionSpec as P

MESH = pl.DeviceIdType.MESH
F32 = jnp.float32
BF16 = jnp.bfloat16
PACK = 16
LANE = 128
TRIAL = 128
LONE = 56


def nt(a, b):
    return lax.dot_general(a, b, (((1,), (1,)), ((), ())), preferred_element_type=F32)


def nn(a, b):
    return lax.dot_general(a, b, (((1,), (0,)), ((), ())), preferred_element_type=F32)


def tn(a, b):
    return lax.dot_general(a, b, (((0,), (0,)), ((), ())), preferred_element_type=F32)


def kernel_of(exchange, cot):
    rows = lax.broadcasted_iota(jnp.int32, exchange.shape, 0)
    cols = lax.broadcasted_iota(jnp.int32, exchange.shape, 1)
    diagonal = rows == cols
    coulomb = jnp.sum(jnp.where(diagonal, exchange, 0.0))
    return (cot * (jnp.where(diagonal, coulomb, 0.0) - exchange)).astype(BF16)


def pack_tail(tail):
    rows, width = tail.shape
    full = rows // PACK * PACK
    blocks = [tail[k:k + PACK] for k in range(0, full, PACK)]
    if full < rows:
        fill = jnp.zeros((full + PACK - rows, width), tail.dtype)
        blocks.append(jnp.concatenate([tail[full:], fill], axis=0))
    return jnp.concatenate(blocks, axis=1)


def unpack_tail(packed, rows, width):
    blocks = []
    for k, start in enumerate(range(0, rows, PACK)):
        count = min(PACK, rows - start)
        blocks.append(packed[:count, k * width:(k + 1) * width])
    return jnp.concatenate(blocks, axis=0)


def put(box, index, piece):
    main = box.shape[2]
    rows, width = piece.shape
    box[index, PACK:, :] = piece[:, :main].astype(box.dtype)
    packed = pack_tail(piece[:, main:])
    box[index, :PACK, :packed.shape[1]] = packed.astype(box.dtype)


def put_trial(box, value):
    rows, lanes = value.shape
    box[TRIAL:, :] = value[:, :LANE].astype(box.dtype)
    middle = value[:, LANE:LANE + LANE // 2].astype(box.dtype)
    split = TRIAL - PACK
    box[PACK:TRIAL, :LANE // 2] = middle[:split]
    box[PACK:PACK + rows - split, LANE // 2:] = middle[split:]
    packed = pack_tail(value[:, LANE + LANE // 2:])
    box[:PACK, :packed.shape[1]] = packed.astype(box.dtype)


def rest_of_trial(box, rows, lanes):
    split = TRIAL - PACK
    pair = box[PACK:TRIAL, :].astype(F32)
    middle = jnp.concatenate(
        [pair[:, :LANE // 2], pair[:rows - split, LANE // 2:]], axis=0
    )
    tail = unpack_tail(box[:PACK, :].astype(F32), rows, lanes - LANE - LANE // 2)
    return jnp.concatenate([middle, tail], axis=1)


def absorb_rows(target, index, box, slot):
    _, rows, width = target.shape
    count, main = box.shape[1:]
    target[index, rows - count:, :main] += box[slot].astype(F32)


def absorb(target, index, box, slot, first, count):
    _, rows, width = target.shape
    main = box.shape[2]
    if first < PACK:
        tail = unpack_tail(box[slot, :PACK, :].astype(F32), rows, width - main)
        target[index, :, main:] += tail
    low, high = max(first, PACK), first + count
    target[index, low - PACK:high - PACK, :main] += box[slot, low:high, :].astype(F32)


def row_chunks(rows, count):
    step = -(-rows // count // 16) * 16
    starts = [k * step for k in range(count)]
    return [(s, e - s) for s, e in zip(starts, starts[1:] + [rows])]


def body(
    chunks, cot_hbm, green_hbm, chol_hbm, trial_hbm, hamil_hbm,
    dgreen_ref, dchol_ref, dtrial_ref,
    cot_ref, green_ref, chol_ref, trial_ref, hamil_ref,
    quarters, peer_quarters, kernels, peer_kernels,
    held, outbox, inbox, foldbox, chol_out, chol_in, lone_out, lone_in,
    part, part_in, trial_out, trial_in,
    load_sem, quarter_send, quarter_recv, kernel_send, kernel_recv,
    chol_send, chol_recv, lone_send, lone_recv, part_send, part_recv, trial_send, trial_recv, done_send, done_recv,
    z_send, z_recv, fold_send, fold_recv, near, far,
):
    n_walk, n_chol = 4, 4
    walk = lax.axis_index("walk")
    rank = lax.axis_index("chol")
    n_vec, occ, orb = chol_ref.shape
    core = walk % 2
    mate = walk + 1 - 2 * core
    across = (walk + 2) % n_walk
    oblique = n_walk - 1 - walk
    quarter = orb // n_walk
    third = orb // n_chol
    half = hamil_ref.shape[0] // 2
    folds = {(0, 3): 1, (3, 0): 2}

    loads = [
        pltpu.make_async_copy(source, target, load_sem.at[k])
        for k, (source, target) in enumerate((
            (green_hbm.at[0], green_ref), (chol_hbm, chol_ref),
            (trial_hbm, trial_ref), (hamil_hbm, hamil_ref), (cot_hbm, cot_ref),
        ))
    ]
    for load in loads:
        load.start()
    barrier = pltpu.get_barrier_semaphore()
    for device in (mate, across, oblique):
        pl.semaphore_signal(barrier, inc=1, device_id={"walk": device}, device_id_type=MESH)

    def enter_here(r):
        pl.semaphore_wait(barrier, 3 + (r > 0))
        for c, entered in ((r + 1, barrier), (r - 1, near), (r - 2, far)):
            if 0 <= c < n_chol:
                pl.semaphore_signal(
                    entered, inc=1, device_id={"chol": c}, device_id_type=MESH
                )

    def enter(r):
        pl.when(rank == r)(functools.partial(enter_here, r))

    def remote(source, target, send, recv, axis, device):
        return pltpu.make_async_remote_copy(
            source, target, send, recv, device_id={axis: device}, device_id_type=MESH
        )

    def to_mate_quarter(k):
        index = mate if k == 0 else (mate + 2) % n_walk
        return remote(
            quarters.at[index], peer_quarters.at[k], quarter_send.at[k], quarter_recv.at[k],
            "walk", mate,
        )

    def to_mate_kernels():
        return remote(kernels, peer_kernels, kernel_send, kernel_recv, "walk", mate)

    def to_across_chol(g):
        span = pl.ds(0, chol_out.shape[1] - LONE * (g == n_vec - 1))
        return remote(
            chol_out.at[g, span], chol_in.at[g, span], chol_send.at[g], chol_recv.at[g],
            "walk", across,
        )

    def to_lone(k):
        device = across if k == 0 else oblique
        return remote(
            lone_out.at[k], lone_in.at[k], lone_send.at[k], lone_recv.at[k], "walk", device
        )

    def send_lone():
        last = kernels[n_vec - 1][:, occ - LONE:]
        for k, device in enumerate((across, oblique)):
            share = quarters[device][:, :lone_out.shape[2]]
            lone_out[k] = tn(last, share).astype(BF16)
            to_lone(k).start()

    def rows_of(side):
        return pl.ds(pl.multiple_of(side * half, 8), half)

    def to_mate_part():
        return remote(part.at[rows_of(1 - core)], part_in, part_send, part_recv, "walk", mate)

    def to_across_trial():
        return remote(trial_out, trial_in, trial_send, trial_recv, "walk", across)

    def to_mate_done(side):
        span = rows_of(side)
        return remote(
            dtrial_ref.at[span], dtrial_ref.at[span], done_send, done_recv, "walk", mate
        )

    def to_z(r, c, k):
        span = pl.ds(*chunks[k])
        return remote(
            outbox.at[c, span], inbox.at[r, span], z_send.at[c, k], z_recv.at[r, k], "chol", c
        )

    def to_fold(c, k, middle):
        span = pl.ds(*chunks[k])
        return remote(
            outbox.at[c, span], foldbox.at[span], fold_send.at[k], fold_recv.at[k],
            "chol", middle,
        )

    def window(c):
        low = c * third // 128 * 128
        high = min(orb, -(-(c + 1) * third // 128) * 128)
        total = cot * tn(trial_ref[...], hamil_ref[:, low:high])
        for g in range(n_vec):
            total = total + nn(kernels[g], chol_ref[g, :, low:high])
        return total[:, c * third - low:(c + 1) * third - low]

    def held_at(r, c):
        return r in [middle for (_, end), middle in folds.items() if end == c]

    def piece_part(r, c, k):
        if (r, c) in folds:
            return to_fold(c, k, folds[r, c])
        return to_z(r, c, k)

    def make_piece(r, c):
        if held_at(r, c):
            put(held, 0, window(c))
        else:
            put(outbox, c, window(c))

    def start_piece(r, c):
        for k in range(len(chunks)):
            piece_part(r, c, k).start()

    lines = {0: (3, 1, 2), 3: (0, 2, 1)}

    def next_piece(r, turn):
        piece_part(r, lines[r][turn - 1], 2 - turn).wait_send()
        start_piece(r, lines[r][turn])

    for r in range(n_chol - 1):
        enter(r)

    loads[0].wait()
    for q in range(n_walk):
        quarters[q] = green_ref[:, q * quarter:(q + 1) * quarter]
    loads[4].wait()
    cot = cot_ref[walk]
    loads[1].wait()
    for g in range(n_vec):
        kernels[g] = kernel_of(nt(chol_ref[g], green_ref[...]), cot)
    @pl.when(rank == n_chol - 1)
    def _():
        loads[2].wait()
        loads[3].wait()
        make_piece(n_chol - 1, lines[n_chol - 1][0])
        enter_here(n_chol - 1)
        start_piece(n_chol - 1, lines[n_chol - 1][0])

    to_mate_quarter(1).start()
    to_mate_kernels().start()
    to_mate_quarter(0).start()

    for r, c in ((0, 3), (1, 0), (2, 1)):

        @pl.when(rank == r)
        def _():
            loads[2].wait()
            loads[3].wait()
            make_piece(r, c)
            if r == 0:
                pl.semaphore_wait(near, 1)
            start_piece(r, c)

    send_lone()
    part[...] = cot * nt(hamil_ref[...], green_ref[...])
    to_mate_part().start()

    for r, c in ((1, 2), (2, 3), (3, lines[3][1])):

        @pl.when(rank == r)
        def _():
            make_piece(r, c)
            if r not in lines:
                pl.semaphore_wait(near, 1)
                start_piece(r, c)

    def across_chol(g):
        put(
            chol_out, g,
            tn(kernels[g], quarters[across]) + tn(peer_kernels[g], peer_quarters[1]),
        )
        to_across_chol(g).start()

    to_mate_quarter(1).wait_recv()
    to_mate_kernels().wait_recv()
    for g in range(n_vec - 1):
        across_chol(g)

    to_mate_part().wait_recv()
    part_in[...] += part[rows_of(core), :]
    put_trial(trial_out, part_in[...])
    to_across_trial().start()
    across_chol(n_vec - 1)

    for r, order in ((0, lines[0][1:]), (1, (3,)), (2, (0,)), (3, lines[3][2:])):

        @pl.when(rank == r)
        def _():
            for k, c in enumerate(order):
                make_piece(r, c)
                if r == 0 and k == 0:
                    next_piece(r, 1)
            if r < 2:
                pl.semaphore_wait(far, 1)
            if r == 3:
                next_piece(r, 1)

    for (start, end), middle in folds.items():

        @pl.when(rank == middle)
        def _():
            for k, (first, count) in enumerate(chunks):
                span = pl.ds(first, count)
                to_fold(end, k, middle).wait_recv()
                outbox[end, span, :] = (
                    held[0, span, :] + foldbox[span, :].astype(F32)
                ).astype(BF16)
                to_z(middle, end, k).start()

    def receive(r, c):
        for k, (first, count) in enumerate(chunks):
            to_z(c, r, k).wait_recv()
            absorb(dgreen_ref, 0, inbox, c, first, count)

    for r in range(n_chol):

        @pl.when(rank == r)
        def _():
            dgreen_ref[0] = window(r)

    to_mate_quarter(0).wait_recv()
    for g in range(n_vec):
        dchol_ref[g] = tn(kernels[g], quarters[walk]) + tn(peer_kernels[g], peer_quarters[0])

    for r in lines:

        @pl.when(rank == r)
        def _():
            next_piece(r, 2)

    for g in range(n_vec - 1):
        to_across_chol(g).wait_recv()
        absorb(dchol_ref, g, chol_in, g, 0, chol_in.shape[1])

    for r, c in ((0, 1), (1, 2), (2, 1), (3, 2)):

        @pl.when(rank == r)
        def _():
            receive(r, c)

    to_across_trial().wait_recv()
    span = rows_of(core)
    half_rows = trial_in[TRIAL:, :].astype(F32)
    dtrial_ref[span, :LANE] = part_in[:, :LANE] + half_rows
    dtrial_ref[span, LANE:] = part_in[:, LANE:] + rest_of_trial(trial_in, half, occ)
    to_mate_done(core).start()

    g = n_vec - 1
    for k in range(2):
        to_lone(k).wait_recv()
        absorb_rows(dchol_ref, g, lone_in, k)
    to_across_chol(g).wait_recv()
    absorb(dchol_ref, g, chol_in, g, 0, chol_in.shape[1] - LONE)

    for r, order in ((0, (2,)), (1, (0, 3)), (2, (3, 0)), (3, (1,))):

        @pl.when(rank == r)
        def _():
            for c in order:
                receive(r, c)

    to_mate_done(1 - core).wait_recv()

    for k in range(2):
        to_mate_quarter(k).wait_send()
        to_lone(k).wait_send()
    for g in range(n_vec):
        to_across_chol(g).wait_send()
    to_mate_kernels().wait_send()
    to_mate_part().wait_send()
    to_across_trial().wait_send()
    to_mate_done(core).wait_send()
    for r in range(n_chol):

        @pl.when(rank == r)
        def _():
            for c in range(n_chol):
                for k in range(len(chunks)):
                    if c != r and (r not in lines or (c, k) not in ((lines[r][0], 1), (lines[r][1], 0))):
                        piece_part(r, c, k).wait_send()


def write_out(*refs):
    sources, targets, sem = refs[:3], refs[3:6], refs[6]
    copies = [pltpu.make_async_copy(s, t, sem.at[k]) for k, (s, t) in enumerate(zip(sources, targets))]
    for copy in copies:
        copy.start()
    for copy in copies:
        copy.wait()


def fused(green, chol, trial, hamil, energy_cot):
    n_chol = lax.axis_size("chol")
    n_walk = lax.axis_size("walk")
    _, occ, orb = green.shape
    n_vec = chol.shape[0]
    rows = hamil.shape[0]
    packed = (occ + PACK, orb // n_chol // 128 * 128)
    chunks = row_chunks(packed[0], 2)
    vmem = pl.BlockSpec(memory_space=pltpu.VMEM)
    anywhere = pl.BlockSpec(memory_space=pl.ANY)
    dma = pltpu.SemaphoreType.DMA
    shapes = [
        (1, occ, orb // n_chol),
        (n_vec, occ, orb // n_walk),
        (rows, occ),
    ]
    results = pl.pallas_call(
        functools.partial(body, chunks),
        out_shape=tuple(pltpu.VMEM(shape, F32) for shape in shapes),
        in_specs=[anywhere] * 5,
        out_specs=(vmem,) * 3,
        scratch_shapes=[
            pltpu.SMEM(energy_cot.shape, F32),
            pltpu.VMEM((occ, orb), BF16),
            pltpu.VMEM(chol.shape, BF16),
            pltpu.VMEM(trial.shape, BF16),
            pltpu.VMEM(hamil.shape, BF16),
            pltpu.VMEM((n_walk, occ, orb // n_walk), BF16),
            pltpu.VMEM((2, occ, orb // n_walk), BF16),
            pltpu.VMEM((n_vec, occ, occ), BF16),
            pltpu.VMEM((n_vec, occ, occ), BF16),
            pltpu.VMEM((1,) + packed, F32),
            pltpu.VMEM((n_chol,) + packed, BF16),
            pltpu.VMEM((n_chol,) + packed, BF16),
            pltpu.VMEM(packed, BF16),
            pltpu.VMEM((n_vec,) + packed, BF16),
            pltpu.VMEM((n_vec,) + packed, BF16),
            pltpu.VMEM((2, LONE, packed[1]), BF16),
            pltpu.VMEM((2, LONE, packed[1]), BF16),
            pltpu.VMEM((rows, occ), F32),
            pltpu.VMEM((rows // 2, occ), F32),
            pltpu.VMEM((rows // 2 + TRIAL, LANE), BF16),
            pltpu.VMEM((rows // 2 + TRIAL, LANE), BF16),
            dma((5,)), dma((2,)), dma((2,)), dma, dma,
            dma((n_vec,)), dma((n_vec,)), dma((2,)), dma((2,)), dma, dma, dma, dma, dma, dma,
            dma((n_chol, len(chunks))), dma((n_chol, len(chunks))),
            dma((len(chunks),)), dma((len(chunks),)),
            pltpu.SemaphoreType.REGULAR, pltpu.SemaphoreType.REGULAR,
        ],
        compiler_params=pltpu.CompilerParams(
            collective_id=0, has_side_effects=True, vmem_limit_bytes=60 * 1024 * 1024
        ),
    )(energy_cot, green, chol, trial, hamil)
    return pl.pallas_call(
        write_out,
        out_shape=tuple(jax.ShapeDtypeStruct(shape, F32) for shape in shapes),
        in_specs=[anywhere] * 3,
        out_specs=(anywhere,) * 3,
        scratch_shapes=[dma((3,))],
        compiler_params=pltpu.CompilerParams(vmem_limit_bytes=1024 * 1024),
    )(*results)


def shards(green, chol, trial, hamil, energy_cot):
    walk_rank = lax.axis_index("walk")
    walk_rows = green.shape[0]
    cot_own = lax.dynamic_slice_in_dim(energy_cot, walk_rank * walk_rows, walk_rows, 0)
    hrot_part = lax.dot_general(
        trial, hamil, (((0,), (0,)), ((), ())), preferred_element_type=jnp.float32
    )
    identity = jnp.eye(trial.shape[1], dtype=jnp.float32)
    quarter = green.shape[2] // lax.axis_size("walk")
    greens = lax.all_gather(green, "walk", axis=0, tiled=True)
    coulomb = jnp.einsum("cip,wip->cw", chol, greens, preferred_element_type=jnp.float32)
    exchange_mat = jnp.einsum("cip,wjp->cwij", chol, greens, preferred_element_type=jnp.float32)
    kernel_mat = (
        energy_cot[None, :, None, None] * (coulomb[:, :, None, None] * identity - exchange_mat)
    ).astype(jnp.bfloat16)
    kernel_own = lax.dynamic_slice_in_dim(kernel_mat, walk_rank * walk_rows, walk_rows, 1)
    green_part = jnp.einsum("cwij,cjp->wip", kernel_own, chol, preferred_element_type=jnp.float32)
    green_part = green_part + cot_own[:, None, None] * hrot_part[None]
    d_green = lax.psum_scatter(green_part, "chol", scatter_dimension=2, tiled=True)
    green_share = lax.dynamic_slice_in_dim(greens, walk_rank * quarter, quarter, 2)
    d_chol = jnp.einsum(
        "cwji,wjp->cip", kernel_mat, green_share, preferred_element_type=jnp.float32
    )
    gbar = jnp.einsum(
        "w,wip->ip",
        energy_cot,
        greens,
        precision=lax.Precision.HIGHEST,
        preferred_element_type=jnp.float32,
    ).astype(jnp.bfloat16)
    d_trial = lax.dot_general(
        hamil, gbar, (((1,), (1,)), ((), ())), preferred_element_type=jnp.float32
    )
    return (d_green, d_chol, d_trial)


def solution(mesh):
    direct = mesh.shape["walk"] == 4 and mesh.shape["chol"] == 4
    return jax.shard_map(
        fused if direct else shards,
        mesh=mesh,
        in_specs=(
            P(("groups", "walk"), None, None),
            P(("groups", "chol"), None, None),
            P(("groups", "chol"), None),
            P("chol", None),
            P("groups"),
        ),
        out_specs=(
            P(("groups", "walk"), None, "chol"),
            P(("groups", "chol"), None, "walk"),
            P(("groups", "chol"), None),
        ),
        check_vma=False,
    )
```

```python
import functools

import jax
import jax.numpy as jnp
from jax import lax
from jax.experimental import pallas as pl
from jax.experimental.pallas import tpu as pltpu
from jax.sharding import PartitionSpec as P

MESH = pl.DeviceIdType.MESH
F32 = jnp.float32
BF16 = jnp.bfloat16
PACK = 16
LANE = 128
TRIAL = 128
LONE = 56


def nt(a, b):
    return lax.dot_general(a, b, (((1,), (1,)), ((), ())), preferred_element_type=F32)


def nn(a, b):
    return lax.dot_general(a, b, (((1,), (0,)), ((), ())), preferred_element_type=F32)


def tn(a, b):
    return lax.dot_general(a, b, (((0,), (0,)), ((), ())), preferred_element_type=F32)


def kernel_of(exchange, cot):
    rows = lax.broadcasted_iota(jnp.int32, exchange.shape, 0)
    cols = lax.broadcasted_iota(jnp.int32, exchange.shape, 1)
    diagonal = rows == cols
    coulomb = jnp.sum(jnp.where(diagonal, exchange, 0.0))
    return (cot * (jnp.where(diagonal, coulomb, 0.0) - exchange)).astype(BF16)


def pack_tail(tail):
    rows, width = tail.shape
    full = rows // PACK * PACK
    blocks = [tail[k:k + PACK] for k in range(0, full, PACK)]
    if full < rows:
        fill = jnp.zeros((full + PACK - rows, width), tail.dtype)
        blocks.append(jnp.concatenate([tail[full:], fill], axis=0))
    return jnp.concatenate(blocks, axis=1)


def unpack_tail(packed, rows, width):
    blocks = []
    for k, start in enumerate(range(0, rows, PACK)):
        count = min(PACK, rows - start)
        blocks.append(packed[:count, k * width:(k + 1) * width])
    return jnp.concatenate(blocks, axis=0)


def put(box, index, piece):
    main = box.shape[2]
    rows, width = piece.shape
    box[index, PACK:, :] = piece[:, :main].astype(box.dtype)
    packed = pack_tail(piece[:, main:])
    box[index, :PACK, :packed.shape[1]] = packed.astype(box.dtype)


def put_trial(box, value):
    rows, lanes = value.shape
    box[TRIAL:, :] = value[:, :LANE].astype(box.dtype)
    middle = value[:, LANE:LANE + LANE // 2].astype(box.dtype)
    split = TRIAL - PACK
    box[PACK:TRIAL, :LANE // 2] = middle[:split]
    box[PACK:PACK + rows - split, LANE // 2:] = middle[split:]
    packed = pack_tail(value[:, LANE + LANE // 2:])
    box[:PACK, :packed.shape[1]] = packed.astype(box.dtype)


def rest_of_trial(box, rows, lanes):
    split = TRIAL - PACK
    pair = box[PACK:TRIAL, :].astype(F32)
    middle = jnp.concatenate(
        [pair[:, :LANE // 2], pair[:rows - split, LANE // 2:]], axis=0
    )
    tail = unpack_tail(box[:PACK, :].astype(F32), rows, lanes - LANE - LANE // 2)
    return jnp.concatenate([middle, tail], axis=1)


def absorb_rows(target, index, box, slot):
    _, rows, width = target.shape
    count, main = box.shape[1:]
    target[index, rows - count:, :main] += box[slot].astype(F32)


def absorb(target, index, box, slot, first, count):
    _, rows, width = target.shape
    main = box.shape[2]
    if first < PACK:
        tail = unpack_tail(box[slot, :PACK, :].astype(F32), rows, width - main)
        target[index, :, main:] += tail
    low, high = max(first, PACK), first + count
    target[index, low - PACK:high - PACK, :main] += box[slot, low:high, :].astype(F32)


def row_chunks(rows, count):
    step = -(-rows // count // 16) * 16
    starts = [k * step for k in range(count)]
    return [(s, e - s) for s, e in zip(starts, starts[1:] + [rows])]


def body(
    chunks, cot_hbm, green_hbm, chol_hbm, trial_hbm, hamil_hbm,
    dgreen_ref, dchol_ref, dtrial_ref,
    cot_ref, green_ref, chol_ref, trial_ref, hamil_ref,
    quarters, peer_quarters, kernels, peer_kernels,
    held, outbox, inbox, foldbox, chol_out, chol_in, lone_out, lone_in,
    part, part_in, trial_out, trial_in,
    load_sem, quarter_send, quarter_recv, kernel_send, kernel_recv,
    chol_send, chol_recv, lone_send, lone_recv, part_send, part_recv, trial_send, trial_recv, done_send, done_recv,
    z_send, z_recv, fold_send, fold_recv, near, far,
):
    n_walk, n_chol = 4, 4
    walk = lax.axis_index("walk")
    rank = lax.axis_index("chol")
    n_vec, occ, orb = chol_ref.shape
    core = walk % 2
    mate = walk + 1 - 2 * core
    across = (walk + 2) % n_walk
    oblique = n_walk - 1 - walk
    quarter = orb // n_walk
    third = orb // n_chol
    half = hamil_ref.shape[0] // 2
    folds = {(0, 3): 1, (3, 0): 2}

    loads = [
        pltpu.make_async_copy(source, target, load_sem.at[k])
        for k, (source, target) in enumerate((
            (green_hbm.at[0], green_ref), (chol_hbm, chol_ref),
            (trial_hbm, trial_ref), (hamil_hbm, hamil_ref), (cot_hbm, cot_ref),
        ))
    ]
    for load in loads:
        load.start()
    barrier = pltpu.get_barrier_semaphore()
    for device in (mate, across, oblique):
        pl.semaphore_signal(barrier, inc=1, device_id={"walk": device}, device_id_type=MESH)

    def enter_here(r):
        pl.semaphore_wait(barrier, 3 + (r > 0))
        for c, entered in ((r + 1, barrier), (r - 1, near), (r - 2, far)):
            if 0 <= c < n_chol:
                pl.semaphore_signal(
                    entered, inc=1, device_id={"chol": c}, device_id_type=MESH
                )

    def enter(r):
        pl.when(rank == r)(functools.partial(enter_here, r))

    def remote(source, target, send, recv, axis, device):
        return pltpu.make_async_remote_copy(
            source, target, send, recv, device_id={axis: device}, device_id_type=MESH
        )

    def to_mate_quarter(k):
        index = mate if k == 0 else (mate + 2) % n_walk
        return remote(
            quarters.at[index], peer_quarters.at[k], quarter_send.at[k], quarter_recv.at[k],
            "walk", mate,
        )

    def to_mate_kernels():
        return remote(kernels, peer_kernels, kernel_send, kernel_recv, "walk", mate)

    def to_across_chol(g):
        span = pl.ds(0, chol_out.shape[1] - LONE * (g == n_vec - 1))
        return remote(
            chol_out.at[g, span], chol_in.at[g, span], chol_send.at[g], chol_recv.at[g],
            "walk", across,
        )

    def to_lone(k):
        device = across if k == 0 else oblique
        return remote(
            lone_out.at[k], lone_in.at[k], lone_send.at[k], lone_recv.at[k], "walk", device
        )

    def send_lone():
        last = kernels[n_vec - 1][:, occ - LONE:]
        for k, device in enumerate((across, oblique)):
            share = quarters[device][:, :lone_out.shape[2]]
            lone_out[k] = tn(last, share).astype(BF16)
            to_lone(k).start()

    def rows_of(side):
        return pl.ds(pl.multiple_of(side * half, 8), half)

    def to_mate_part():
        return remote(part.at[rows_of(1 - core)], part_in, part_send, part_recv, "walk", mate)

    def to_across_trial():
        return remote(trial_out, trial_in, trial_send, trial_recv, "walk", across)

    def to_mate_done(side):
        span = rows_of(side)
        return remote(
            dtrial_ref.at[span], dtrial_ref.at[span], done_send, done_recv, "walk", mate
        )

    def to_z(r, c, k):
        span = pl.ds(*chunks[k])
        return remote(
            outbox.at[c, span], inbox.at[r, span], z_send.at[c, k], z_recv.at[r, k], "chol", c
        )

    def to_fold(c, k, middle):
        span = pl.ds(*chunks[k])
        return remote(
            outbox.at[c, span], foldbox.at[span], fold_send.at[k], fold_recv.at[k],
            "chol", middle,
        )

    def window(c):
        low = c * third // 128 * 128
        high = min(orb, -(-(c + 1) * third // 128) * 128)
        total = cot * tn(trial_ref[...], hamil_ref[:, low:high])
        for g in range(n_vec):
            total = total + nn(kernels[g], chol_ref[g, :, low:high])
        return total[:, c * third - low:(c + 1) * third - low]

    def held_at(r, c):
        return r in [middle for (_, end), middle in folds.items() if end == c]

    def piece_part(r, c, k):
        if (r, c) in folds:
            return to_fold(c, k, folds[r, c])
        return to_z(r, c, k)

    def make_piece(r, c):
        if held_at(r, c):
            put(held, 0, window(c))
        else:
            put(outbox, c, window(c))

    def start_piece(r, c):
        for k in range(len(chunks)):
            piece_part(r, c, k).start()

    lines = {0: (3, 1, 2), 3: (0, 2, 1)}

    def next_piece(r, turn):
        piece_part(r, lines[r][turn - 1], 2 - turn).wait_send()
        start_piece(r, lines[r][turn])

    for r in range(n_chol - 1):
        enter(r)

    loads[0].wait()
    for q in range(n_walk):
        quarters[q] = green_ref[:, q * quarter:(q + 1) * quarter]
    loads[4].wait()
    cot = cot_ref[walk]
    loads[1].wait()
    for g in range(n_vec):
        kernels[g] = kernel_of(nt(chol_ref[g], green_ref[...]), cot)
    @pl.when(rank == n_chol - 1)
    def _():
        loads[2].wait()
        loads[3].wait()
        make_piece(n_chol - 1, lines[n_chol - 1][0])
        enter_here(n_chol - 1)
        start_piece(n_chol - 1, lines[n_chol - 1][0])

    to_mate_quarter(1).start()
    to_mate_kernels().start()
    to_mate_quarter(0).start()
    pl.when(rank == 0)(send_lone)

    for r, c in ((0, 3), (1, 0), (2, 1)):

        @pl.when(rank == r)
        def _():
            loads[2].wait()
            loads[3].wait()
            make_piece(r, c)
            if r == 0:
                pl.semaphore_wait(near, 1)
            start_piece(r, c)

    pl.when(rank > 0)(send_lone)
    part[...] = cot * nt(hamil_ref[...], green_ref[...])
    to_mate_part().start()

    for r, c in ((1, 2), (2, 3), (3, lines[3][1])):

        @pl.when(rank == r)
        def _():
            make_piece(r, c)
            if r not in lines:
                pl.semaphore_wait(near, 1)
                start_piece(r, c)

    def across_chol(g):
        put(
            chol_out, g,
            tn(kernels[g], quarters[across]) + tn(peer_kernels[g], peer_quarters[1]),
        )
        to_across_chol(g).start()

    to_mate_quarter(1).wait_recv()
    to_mate_kernels().wait_recv()
    for g in range(n_vec - 1):
        across_chol(g)

    to_mate_part().wait_recv()
    part_in[...] += part[rows_of(core), :]
    put_trial(trial_out, part_in[...])
    to_across_trial().start()
    across_chol(n_vec - 1)

    for r, order in ((0, lines[0][1:]), (1, (3,)), (2, (0,)), (3, lines[3][2:])):

        @pl.when(rank == r)
        def _():
            for k, c in enumerate(order):
                make_piece(r, c)
                if r == 0 and k == 0:
                    next_piece(r, 1)
            if r < 2:
                pl.semaphore_wait(far, 1)
            if r == 3:
                next_piece(r, 1)

    for (start, end), middle in folds.items():

        @pl.when(rank == middle)
        def _():
            for k, (first, count) in enumerate(chunks):
                span = pl.ds(first, count)
                to_fold(end, k, middle).wait_recv()
                outbox[end, span, :] = (
                    held[0, span, :] + foldbox[span, :].astype(F32)
                ).astype(BF16)
                to_z(middle, end, k).start()

    def receive(r, c):
        for k, (first, count) in enumerate(chunks):
            to_z(c, r, k).wait_recv()
            absorb(dgreen_ref, 0, inbox, c, first, count)

    for r in range(n_chol):

        @pl.when(rank == r)
        def _():
            dgreen_ref[0] = window(r)

    to_mate_quarter(0).wait_recv()
    for g in range(n_vec):
        dchol_ref[g] = tn(kernels[g], quarters[walk]) + tn(peer_kernels[g], peer_quarters[0])

    for r in lines:

        @pl.when(rank == r)
        def _():
            next_piece(r, 2)

    for g in range(n_vec - 1):
        to_across_chol(g).wait_recv()
        absorb(dchol_ref, g, chol_in, g, 0, chol_in.shape[1])

    for r, c in ((0, 1), (1, 2), (2, 1), (3, 2)):

        @pl.when(rank == r)
        def _():
            receive(r, c)

    to_across_trial().wait_recv()
    span = rows_of(core)
    half_rows = trial_in[TRIAL:, :].astype(F32)
    dtrial_ref[span, :LANE] = part_in[:, :LANE] + half_rows
    dtrial_ref[span, LANE:] = part_in[:, LANE:] + rest_of_trial(trial_in, half, occ)
    to_mate_done(core).start()

    g = n_vec - 1
    for k in range(2):
        to_lone(k).wait_recv()
        absorb_rows(dchol_ref, g, lone_in, k)
    to_across_chol(g).wait_recv()
    absorb(dchol_ref, g, chol_in, g, 0, chol_in.shape[1] - LONE)

    for r, order in ((0, (2,)), (1, (0, 3)), (2, (3, 0)), (3, (1,))):

        @pl.when(rank == r)
        def _():
            for c in order:
                receive(r, c)

    to_mate_done(1 - core).wait_recv()

    for k in range(2):
        to_mate_quarter(k).wait_send()
        to_lone(k).wait_send()
    for g in range(n_vec):
        to_across_chol(g).wait_send()
    to_mate_kernels().wait_send()
    to_mate_part().wait_send()
    to_across_trial().wait_send()
    to_mate_done(core).wait_send()
    for r in range(n_chol):

        @pl.when(rank == r)
        def _():
            for c in range(n_chol):
                for k in range(len(chunks)):
                    if c != r and (r not in lines or (c, k) not in ((lines[r][0], 1), (lines[r][1], 0))):
                        piece_part(r, c, k).wait_send()


def write_out(*refs):
    sources, targets, sem = refs[:3], refs[3:6], refs[6]
    copies = [pltpu.make_async_copy(s, t, sem.at[k]) for k, (s, t) in enumerate(zip(sources, targets))]
    for copy in copies:
        copy.start()
    for copy in copies:
        copy.wait()


def fused(green, chol, trial, hamil, energy_cot):
    n_chol = lax.axis_size("chol")
    n_walk = lax.axis_size("walk")
    _, occ, orb = green.shape
    n_vec = chol.shape[0]
    rows = hamil.shape[0]
    packed = (occ + PACK, orb // n_chol // 128 * 128)
    chunks = row_chunks(packed[0], 2)
    vmem = pl.BlockSpec(memory_space=pltpu.VMEM)
    anywhere = pl.BlockSpec(memory_space=pl.ANY)
    dma = pltpu.SemaphoreType.DMA
    shapes = [
        (1, occ, orb // n_chol),
        (n_vec, occ, orb // n_walk),
        (rows, occ),
    ]
    results = pl.pallas_call(
        functools.partial(body, chunks),
        out_shape=tuple(pltpu.VMEM(shape, F32) for shape in shapes),
        in_specs=[anywhere] * 5,
        out_specs=(vmem,) * 3,
        scratch_shapes=[
            pltpu.SMEM(energy_cot.shape, F32),
            pltpu.VMEM((occ, orb), BF16),
            pltpu.VMEM(chol.shape, BF16),
            pltpu.VMEM(trial.shape, BF16),
            pltpu.VMEM(hamil.shape, BF16),
            pltpu.VMEM((n_walk, occ, orb // n_walk), BF16),
            pltpu.VMEM((2, occ, orb // n_walk), BF16),
            pltpu.VMEM((n_vec, occ, occ), BF16),
            pltpu.VMEM((n_vec, occ, occ), BF16),
            pltpu.VMEM((1,) + packed, F32),
            pltpu.VMEM((n_chol,) + packed, BF16),
            pltpu.VMEM((n_chol,) + packed, BF16),
            pltpu.VMEM(packed, BF16),
            pltpu.VMEM((n_vec,) + packed, BF16),
            pltpu.VMEM((n_vec,) + packed, BF16),
            pltpu.VMEM((2, LONE, packed[1]), BF16),
            pltpu.VMEM((2, LONE, packed[1]), BF16),
            pltpu.VMEM((rows, occ), F32),
            pltpu.VMEM((rows // 2, occ), F32),
            pltpu.VMEM((rows // 2 + TRIAL, LANE), BF16),
            pltpu.VMEM((rows // 2 + TRIAL, LANE), BF16),
            dma((5,)), dma((2,)), dma((2,)), dma, dma,
            dma((n_vec,)), dma((n_vec,)), dma((2,)), dma((2,)), dma, dma, dma, dma, dma, dma,
            dma((n_chol, len(chunks))), dma((n_chol, len(chunks))),
            dma((len(chunks),)), dma((len(chunks),)),
            pltpu.SemaphoreType.REGULAR, pltpu.SemaphoreType.REGULAR,
        ],
        compiler_params=pltpu.CompilerParams(
            collective_id=0, has_side_effects=True, vmem_limit_bytes=60 * 1024 * 1024
        ),
    )(energy_cot, green, chol, trial, hamil)
    return pl.pallas_call(
        write_out,
        out_shape=tuple(jax.ShapeDtypeStruct(shape, F32) for shape in shapes),
        in_specs=[anywhere] * 3,
        out_specs=(anywhere,) * 3,
        scratch_shapes=[dma((3,))],
        compiler_params=pltpu.CompilerParams(vmem_limit_bytes=1024 * 1024),
    )(*results)


def shards(green, chol, trial, hamil, energy_cot):
    walk_rank = lax.axis_index("walk")
    walk_rows = green.shape[0]
    cot_own = lax.dynamic_slice_in_dim(energy_cot, walk_rank * walk_rows, walk_rows, 0)
    hrot_part = lax.dot_general(
        trial, hamil, (((0,), (0,)), ((), ())), preferred_element_type=jnp.float32
    )
    identity = jnp.eye(trial.shape[1], dtype=jnp.float32)
    quarter = green.shape[2] // lax.axis_size("walk")
    greens = lax.all_gather(green, "walk", axis=0, tiled=True)
    coulomb = jnp.einsum("cip,wip->cw", chol, greens, preferred_element_type=jnp.float32)
    exchange_mat = jnp.einsum("cip,wjp->cwij", chol, greens, preferred_element_type=jnp.float32)
    kernel_mat = (
        energy_cot[None, :, None, None] * (coulomb[:, :, None, None] * identity - exchange_mat)
    ).astype(jnp.bfloat16)
    kernel_own = lax.dynamic_slice_in_dim(kernel_mat, walk_rank * walk_rows, walk_rows, 1)
    green_part = jnp.einsum("cwij,cjp->wip", kernel_own, chol, preferred_element_type=jnp.float32)
    green_part = green_part + cot_own[:, None, None] * hrot_part[None]
    d_green = lax.psum_scatter(green_part, "chol", scatter_dimension=2, tiled=True)
    green_share = lax.dynamic_slice_in_dim(greens, walk_rank * quarter, quarter, 2)
    d_chol = jnp.einsum(
        "cwji,wjp->cip", kernel_mat, green_share, preferred_element_type=jnp.float32
    )
    gbar = jnp.einsum(
        "w,wip->ip",
        energy_cot,
        greens,
        precision=lax.Precision.HIGHEST,
        preferred_element_type=jnp.float32,
    ).astype(jnp.bfloat16)
    d_trial = lax.dot_general(
        hamil, gbar, (((1,), (1,)), ((), ())), preferred_element_type=jnp.float32
    )
    return (d_green, d_chol, d_trial)


def solution(mesh):
    direct = mesh.shape["walk"] == 4 and mesh.shape["chol"] == 4
    return jax.shard_map(
        fused if direct else shards,
        mesh=mesh,
        in_specs=(
            P(("groups", "walk"), None, None),
            P(("groups", "chol"), None, None),
            P(("groups", "chol"), None),
            P("chol", None),
            P("groups"),
        ),
        out_specs=(
            P(("groups", "walk"), None, "chol"),
            P(("groups", "chol"), None, "walk"),
            P(("groups", "chol"), None),
        ),
        check_vma=False,
    )
```

```python
import functools

import jax
import jax.numpy as jnp
from jax import lax
from jax.experimental import pallas as pl
from jax.experimental.pallas import tpu as pltpu
from jax.sharding import PartitionSpec as P

MESH = pl.DeviceIdType.MESH
F32 = jnp.float32
BF16 = jnp.bfloat16
PACK = 16
LANE = 128
TRIAL = 128
LONE = 72


def nt(a, b):
    return lax.dot_general(a, b, (((1,), (1,)), ((), ())), preferred_element_type=F32)


def nn(a, b):
    return lax.dot_general(a, b, (((1,), (0,)), ((), ())), preferred_element_type=F32)


def tn(a, b):
    return lax.dot_general(a, b, (((0,), (0,)), ((), ())), preferred_element_type=F32)


def kernel_of(exchange, cot):
    rows = lax.broadcasted_iota(jnp.int32, exchange.shape, 0)
    cols = lax.broadcasted_iota(jnp.int32, exchange.shape, 1)
    diagonal = rows == cols
    coulomb = jnp.sum(jnp.where(diagonal, exchange, 0.0))
    return (cot * (jnp.where(diagonal, coulomb, 0.0) - exchange)).astype(BF16)


def pack_tail(tail):
    rows, width = tail.shape
    full = rows // PACK * PACK
    blocks = [tail[k:k + PACK] for k in range(0, full, PACK)]
    if full < rows:
        fill = jnp.zeros((full + PACK - rows, width), tail.dtype)
        blocks.append(jnp.concatenate([tail[full:], fill], axis=0))
    return jnp.concatenate(blocks, axis=1)


def unpack_tail(packed, rows, width):
    blocks = []
    for k, start in enumerate(range(0, rows, PACK)):
        count = min(PACK, rows - start)
        blocks.append(packed[:count, k * width:(k + 1) * width])
    return jnp.concatenate(blocks, axis=0)


def put(box, index, piece):
    main = box.shape[2]
    rows, width = piece.shape
    box[index, PACK:, :] = piece[:, :main].astype(box.dtype)
    packed = pack_tail(piece[:, main:])
    box[index, :PACK, :packed.shape[1]] = packed.astype(box.dtype)


def put_trial(box, value):
    rows, lanes = value.shape
    box[TRIAL:, :] = value[:, :LANE].astype(box.dtype)
    middle = value[:, LANE:LANE + LANE // 2].astype(box.dtype)
    split = TRIAL - PACK
    box[PACK:TRIAL, :LANE // 2] = middle[:split]
    box[PACK:PACK + rows - split, LANE // 2:] = middle[split:]
    packed = pack_tail(value[:, LANE + LANE // 2:])
    box[:PACK, :packed.shape[1]] = packed.astype(box.dtype)


def rest_of_trial(box, rows, lanes):
    split = TRIAL - PACK
    pair = box[PACK:TRIAL, :].astype(F32)
    middle = jnp.concatenate(
        [pair[:, :LANE // 2], pair[:rows - split, LANE // 2:]], axis=0
    )
    tail = unpack_tail(box[:PACK, :].astype(F32), rows, lanes - LANE - LANE // 2)
    return jnp.concatenate([middle, tail], axis=1)


def absorb_rows(target, index, box, slot):
    _, rows, width = target.shape
    count, main = box.shape[1:]
    target[index, rows - count:, :main] += box[slot].astype(F32)


def absorb(target, index, box, slot, first, count):
    _, rows, width = target.shape
    main = box.shape[2]
    if first < PACK:
        tail = unpack_tail(box[slot, :PACK, :].astype(F32), rows, width - main)
        target[index, :, main:] += tail
    low, high = max(first, PACK), first + count
    target[index, low - PACK:high - PACK, :main] += box[slot, low:high, :].astype(F32)


def row_chunks(rows, count):
    step = -(-rows // count // 16) * 16
    starts = [k * step for k in range(count)]
    return [(s, e - s) for s, e in zip(starts, starts[1:] + [rows])]


def body(
    chunks, cot_hbm, green_hbm, chol_hbm, trial_hbm, hamil_hbm,
    dgreen_ref, dchol_ref, dtrial_ref,
    cot_ref, green_ref, chol_ref, trial_ref, hamil_ref,
    quarters, peer_quarters, kernels, peer_kernels,
    held, outbox, inbox, foldbox, chol_out, chol_in, lone_out, lone_in,
    part, part_in, trial_out, trial_in,
    load_sem, quarter_send, quarter_recv, kernel_send, kernel_recv,
    chol_send, chol_recv, lone_send, lone_recv, part_send, part_recv, trial_send, trial_recv, done_send, done_recv,
    z_send, z_recv, fold_send, fold_recv, near, far,
):
    n_walk, n_chol = 4, 4
    walk = lax.axis_index("walk")
    rank = lax.axis_index("chol")
    n_vec, occ, orb = chol_ref.shape
    core = walk % 2
    mate = walk + 1 - 2 * core
    across = (walk + 2) % n_walk
    oblique = n_walk - 1 - walk
    quarter = orb // n_walk
    third = orb // n_chol
    half = hamil_ref.shape[0] // 2
    folds = {(0, 3): 1, (3, 0): 2}

    loads = [
        pltpu.make_async_copy(source, target, load_sem.at[k])
        for k, (source, target) in enumerate((
            (green_hbm.at[0], green_ref), (chol_hbm, chol_ref),
            (trial_hbm, trial_ref), (hamil_hbm, hamil_ref), (cot_hbm, cot_ref),
        ))
    ]
    for load in loads:
        load.start()
    barrier = pltpu.get_barrier_semaphore()
    for device in (mate, across, oblique):
        pl.semaphore_signal(barrier, inc=1, device_id={"walk": device}, device_id_type=MESH)

    def enter_here(r):
        pl.semaphore_wait(barrier, 3 + (r > 0))
        for c, entered in ((r + 1, barrier), (r - 1, near), (r - 2, far)):
            if 0 <= c < n_chol:
                pl.semaphore_signal(
                    entered, inc=1, device_id={"chol": c}, device_id_type=MESH
                )

    def enter(r):
        pl.when(rank == r)(functools.partial(enter_here, r))

    def remote(source, target, send, recv, axis, device):
        return pltpu.make_async_remote_copy(
            source, target, send, recv, device_id={axis: device}, device_id_type=MESH
        )

    def to_mate_quarter(k):
        index = mate if k == 0 else (mate + 2) % n_walk
        return remote(
            quarters.at[index], peer_quarters.at[k], quarter_send.at[k], quarter_recv.at[k],
            "walk", mate,
        )

    def to_mate_kernels():
        return remote(kernels, peer_kernels, kernel_send, kernel_recv, "walk", mate)

    def to_across_chol(g):
        span = pl.ds(0, chol_out.shape[1] - LONE * (g == n_vec - 1))
        return remote(
            chol_out.at[g, span], chol_in.at[g, span], chol_send.at[g], chol_recv.at[g],
            "walk", across,
        )

    def to_lone(k):
        device = across if k == 0 else oblique
        return remote(
            lone_out.at[k], lone_in.at[k], lone_send.at[k], lone_recv.at[k], "walk", device
        )

    def send_lone():
        last = kernels[n_vec - 1][:, occ - LONE:]
        for k, device in enumerate((across, oblique)):
            share = quarters[device][:, :lone_out.shape[2]]
            lone_out[k] = tn(last, share).astype(BF16)
            to_lone(k).start()

    def rows_of(side):
        return pl.ds(pl.multiple_of(side * half, 8), half)

    def to_mate_part():
        return remote(part.at[rows_of(1 - core)], part_in, part_send, part_recv, "walk", mate)

    def to_across_trial():
        return remote(trial_out, trial_in, trial_send, trial_recv, "walk", across)

    def to_mate_done(side):
        span = rows_of(side)
        return remote(
            dtrial_ref.at[span], dtrial_ref.at[span], done_send, done_recv, "walk", mate
        )

    def to_z(r, c, k):
        span = pl.ds(*chunks[k])
        return remote(
            outbox.at[c, span], inbox.at[r, span], z_send.at[c, k], z_recv.at[r, k], "chol", c
        )

    def to_fold(c, k, middle):
        span = pl.ds(*chunks[k])
        return remote(
            outbox.at[c, span], foldbox.at[span], fold_send.at[k], fold_recv.at[k],
            "chol", middle,
        )

    def window(c):
        low = c * third // 128 * 128
        high = min(orb, -(-(c + 1) * third // 128) * 128)
        total = cot * tn(trial_ref[...], hamil_ref[:, low:high])
        for g in range(n_vec):
            total = total + nn(kernels[g], chol_ref[g, :, low:high])
        return total[:, c * third - low:(c + 1) * third - low]

    def held_at(r, c):
        return r in [middle for (_, end), middle in folds.items() if end == c]

    def piece_part(r, c, k):
        if (r, c) in folds:
            return to_fold(c, k, folds[r, c])
        return to_z(r, c, k)

    def make_piece(r, c):
        if held_at(r, c):
            put(held, 0, window(c))
        else:
            put(outbox, c, window(c))

    def start_piece(r, c):
        for k in range(len(chunks)):
            piece_part(r, c, k).start()

    lines = {0: (3, 1, 2), 3: (0, 2, 1)}

    def next_piece(r, turn):
        piece_part(r, lines[r][turn - 1], 2 - turn).wait_send()
        start_piece(r, lines[r][turn])

    for r in range(n_chol - 1):
        enter(r)

    loads[0].wait()
    for q in range(n_walk):
        quarters[q] = green_ref[:, q * quarter:(q + 1) * quarter]
    loads[4].wait()
    cot = cot_ref[walk]
    loads[1].wait()
    for g in range(n_vec):
        kernels[g] = kernel_of(nt(chol_ref[g], green_ref[...]), cot)
    @pl.when(rank == n_chol - 1)
    def _():
        loads[2].wait()
        loads[3].wait()
        make_piece(n_chol - 1, lines[n_chol - 1][0])
        enter_here(n_chol - 1)
        start_piece(n_chol - 1, lines[n_chol - 1][0])

    to_mate_quarter(1).start()
    to_mate_kernels().start()
    to_mate_quarter(0).start()
    pl.when(rank == 0)(send_lone)

    for r, c in ((0, 3), (1, 0), (2, 1)):

        @pl.when(rank == r)
        def _():
            loads[2].wait()
            loads[3].wait()
            make_piece(r, c)
            if r == 0:
                pl.semaphore_wait(near, 1)
            start_piece(r, c)

    pl.when(rank > 0)(send_lone)
    part[...] = cot * nt(hamil_ref[...], green_ref[...])
    to_mate_part().start()

    for r, c in ((1, 2), (2, 3), (3, lines[3][1])):

        @pl.when(rank == r)
        def _():
            make_piece(r, c)
            if r not in lines:
                pl.semaphore_wait(near, 1)
                start_piece(r, c)

    def across_chol(g):
        put(
            chol_out, g,
            tn(kernels[g], quarters[across]) + tn(peer_kernels[g], peer_quarters[1]),
        )
        to_across_chol(g).start()

    to_mate_quarter(1).wait_recv()
    to_mate_kernels().wait_recv()
    for g in range(n_vec - 1):
        across_chol(g)

    to_mate_part().wait_recv()
    part_in[...] += part[rows_of(core), :]
    put_trial(trial_out, part_in[...])
    to_across_trial().start()
    across_chol(n_vec - 1)

    for r, order in ((0, lines[0][1:]), (1, (3,)), (2, (0,)), (3, lines[3][2:])):

        @pl.when(rank == r)
        def _():
            for k, c in enumerate(order):
                make_piece(r, c)
                if r == 0 and k == 0:
                    next_piece(r, 1)
            if r < 2:
                pl.semaphore_wait(far, 1)
            if r == 3:
                next_piece(r, 1)

    for (start, end), middle in folds.items():

        @pl.when(rank == middle)
        def _():
            for k, (first, count) in enumerate(chunks):
                span = pl.ds(first, count)
                to_fold(end, k, middle).wait_recv()
                outbox[end, span, :] = (
                    held[0, span, :] + foldbox[span, :].astype(F32)
                ).astype(BF16)
                to_z(middle, end, k).start()

    def receive(r, c):
        for k, (first, count) in enumerate(chunks):
            to_z(c, r, k).wait_recv()
            absorb(dgreen_ref, 0, inbox, c, first, count)

    for r in range(n_chol):

        @pl.when(rank == r)
        def _():
            dgreen_ref[0] = window(r)

    to_mate_quarter(0).wait_recv()
    for g in range(n_vec):
        dchol_ref[g] = tn(kernels[g], quarters[walk]) + tn(peer_kernels[g], peer_quarters[0])

    for r in lines:

        @pl.when(rank == r)
        def _():
            next_piece(r, 2)

    for g in range(n_vec - 1):
        to_across_chol(g).wait_recv()
        absorb(dchol_ref, g, chol_in, g, 0, chol_in.shape[1])

    for r, c in ((0, 1), (1, 2), (2, 1), (3, 2)):

        @pl.when(rank == r)
        def _():
            receive(r, c)

    to_across_trial().wait_recv()
    span = rows_of(core)
    half_rows = trial_in[TRIAL:, :].astype(F32)
    dtrial_ref[span, :LANE] = part_in[:, :LANE] + half_rows
    dtrial_ref[span, LANE:] = part_in[:, LANE:] + rest_of_trial(trial_in, half, occ)
    to_mate_done(core).start()

    g = n_vec - 1
    for k in range(2):
        to_lone(k).wait_recv()
        absorb_rows(dchol_ref, g, lone_in, k)
    to_across_chol(g).wait_recv()
    absorb(dchol_ref, g, chol_in, g, 0, chol_in.shape[1] - LONE)

    for r, order in ((0, (2,)), (1, (0, 3)), (2, (3, 0)), (3, (1,))):

        @pl.when(rank == r)
        def _():
            for c in order:
                receive(r, c)

    to_mate_done(1 - core).wait_recv()

    for k in range(2):
        to_mate_quarter(k).wait_send()
        to_lone(k).wait_send()
    for g in range(n_vec):
        to_across_chol(g).wait_send()
    to_mate_kernels().wait_send()
    to_mate_part().wait_send()
    to_across_trial().wait_send()
    to_mate_done(core).wait_send()
    for r in range(n_chol):

        @pl.when(rank == r)
        def _():
            for c in range(n_chol):
                for k in range(len(chunks)):
                    if c != r and (r not in lines or (c, k) not in ((lines[r][0], 1), (lines[r][1], 0))):
                        piece_part(r, c, k).wait_send()


def write_out(*refs):
    sources, targets, sem = refs[:3], refs[3:6], refs[6]
    copies = [pltpu.make_async_copy(s, t, sem.at[k]) for k, (s, t) in enumerate(zip(sources, targets))]
    for copy in copies:
        copy.start()
    for copy in copies:
        copy.wait()


def fused(green, chol, trial, hamil, energy_cot):
    n_chol = lax.axis_size("chol")
    n_walk = lax.axis_size("walk")
    _, occ, orb = green.shape
    n_vec = chol.shape[0]
    rows = hamil.shape[0]
    packed = (occ + PACK, orb // n_chol // 128 * 128)
    chunks = row_chunks(packed[0], 2)
    vmem = pl.BlockSpec(memory_space=pltpu.VMEM)
    anywhere = pl.BlockSpec(memory_space=pl.ANY)
    dma = pltpu.SemaphoreType.DMA
    shapes = [
        (1, occ, orb // n_chol),
        (n_vec, occ, orb // n_walk),
        (rows, occ),
    ]
    results = pl.pallas_call(
        functools.partial(body, chunks),
        out_shape=tuple(pltpu.VMEM(shape, F32) for shape in shapes),
        in_specs=[anywhere] * 5,
        out_specs=(vmem,) * 3,
        scratch_shapes=[
            pltpu.SMEM(energy_cot.shape, F32),
            pltpu.VMEM((occ, orb), BF16),
            pltpu.VMEM(chol.shape, BF16),
            pltpu.VMEM(trial.shape, BF16),
            pltpu.VMEM(hamil.shape, BF16),
            pltpu.VMEM((n_walk, occ, orb // n_walk), BF16),
            pltpu.VMEM((2, occ, orb // n_walk), BF16),
            pltpu.VMEM((n_vec, occ, occ), BF16),
            pltpu.VMEM((n_vec, occ, occ), BF16),
            pltpu.VMEM((1,) + packed, F32),
            pltpu.VMEM((n_chol,) + packed, BF16),
            pltpu.VMEM((n_chol,) + packed, BF16),
            pltpu.VMEM(packed, BF16),
            pltpu.VMEM((n_vec,) + packed, BF16),
            pltpu.VMEM((n_vec,) + packed, BF16),
            pltpu.VMEM((2, LONE, packed[1]), BF16),
            pltpu.VMEM((2, LONE, packed[1]), BF16),
            pltpu.VMEM((rows, occ), F32),
            pltpu.VMEM((rows // 2, occ), F32),
            pltpu.VMEM((rows // 2 + TRIAL, LANE), BF16),
            pltpu.VMEM((rows // 2 + TRIAL, LANE), BF16),
            dma((5,)), dma((2,)), dma((2,)), dma, dma,
            dma((n_vec,)), dma((n_vec,)), dma((2,)), dma((2,)), dma, dma, dma, dma, dma, dma,
            dma((n_chol, len(chunks))), dma((n_chol, len(chunks))),
            dma((len(chunks),)), dma((len(chunks),)),
            pltpu.SemaphoreType.REGULAR, pltpu.SemaphoreType.REGULAR,
        ],
        compiler_params=pltpu.CompilerParams(
            collective_id=0, has_side_effects=True, vmem_limit_bytes=60 * 1024 * 1024
        ),
    )(energy_cot, green, chol, trial, hamil)
    return pl.pallas_call(
        write_out,
        out_shape=tuple(jax.ShapeDtypeStruct(shape, F32) for shape in shapes),
        in_specs=[anywhere] * 3,
        out_specs=(anywhere,) * 3,
        scratch_shapes=[dma((3,))],
        compiler_params=pltpu.CompilerParams(vmem_limit_bytes=1024 * 1024),
    )(*results)


def shards(green, chol, trial, hamil, energy_cot):
    walk_rank = lax.axis_index("walk")
    walk_rows = green.shape[0]
    cot_own = lax.dynamic_slice_in_dim(energy_cot, walk_rank * walk_rows, walk_rows, 0)
    hrot_part = lax.dot_general(
        trial, hamil, (((0,), (0,)), ((), ())), preferred_element_type=jnp.float32
    )
    identity = jnp.eye(trial.shape[1], dtype=jnp.float32)
    quarter = green.shape[2] // lax.axis_size("walk")
    greens = lax.all_gather(green, "walk", axis=0, tiled=True)
    coulomb = jnp.einsum("cip,wip->cw", chol, greens, preferred_element_type=jnp.float32)
    exchange_mat = jnp.einsum("cip,wjp->cwij", chol, greens, preferred_element_type=jnp.float32)
    kernel_mat = (
        energy_cot[None, :, None, None] * (coulomb[:, :, None, None] * identity - exchange_mat)
    ).astype(jnp.bfloat16)
    kernel_own = lax.dynamic_slice_in_dim(kernel_mat, walk_rank * walk_rows, walk_rows, 1)
    green_part = jnp.einsum("cwij,cjp->wip", kernel_own, chol, preferred_element_type=jnp.float32)
    green_part = green_part + cot_own[:, None, None] * hrot_part[None]
    d_green = lax.psum_scatter(green_part, "chol", scatter_dimension=2, tiled=True)
    green_share = lax.dynamic_slice_in_dim(greens, walk_rank * quarter, quarter, 2)
    d_chol = jnp.einsum(
        "cwji,wjp->cip", kernel_mat, green_share, preferred_element_type=jnp.float32
    )
    gbar = jnp.einsum(
        "w,wip->ip",
        energy_cot,
        greens,
        precision=lax.Precision.HIGHEST,
        preferred_element_type=jnp.float32,
    ).astype(jnp.bfloat16)
    d_trial = lax.dot_general(
        hamil, gbar, (((1,), (1,)), ((), ())), preferred_element_type=jnp.float32
    )
    return (d_green, d_chol, d_trial)


def solution(mesh):
    direct = mesh.shape["walk"] == 4 and mesh.shape["chol"] == 4
    return jax.shard_map(
        fused if direct else shards,
        mesh=mesh,
        in_specs=(
            P(("groups", "walk"), None, None),
            P(("groups", "chol"), None, None),
            P(("groups", "chol"), None),
            P("chol", None),
            P("groups"),
        ),
        out_specs=(
            P(("groups", "walk"), None, "chol"),
            P(("groups", "chol"), None, "walk"),
            P(("groups", "chol"), None),
        ),
        check_vma=False,
    )
```
